512 devices in a mesh: section: 16 (over z), row: 8 (over y, core), col: 4 (over x).
Axes of the slice: x: 4, y: 4, z: 16, core: 2. Of those that a mesh axis runs over, the one named last changes fastest.
Arguments:
- x_fwd: bfloat16 [4096, 12288], P('section', 'row'), may hold values from -6 to 6
- dy_bwd: bfloat16 [4096, 12288], P(('section', 'row'), 'col'), may hold values from -6 to 6
- w_blocks: bfloat16 [16, 8, 4, 115, 128, 128], P('section', 'row', 'col'), may hold values from -0.09375 to 0.09375
- blk_row: int32 [16, 8, 4, 115], P('section', 'row', 'col'), may hold values from 0 to 11, as said below
- blk_col: int32 [16, 8, 4, 115], P('section', 'row', 'col'), may hold values from 0 to 23, as said below
- blk_count: int32 [16, 8, 4], P('section', 'row', 'col'), may hold values from 57 to 115, as said below
- tok_count: int32 [16, 2], P('section'), may hold values from 64 to 256, as said below
- owner_order: int32 [16, 64], P('section'), may hold values from 0 to 63, each once within a row
Outputs:
- y_next: bfloat16 [4096, 12288], P(('section', 'row', 'col'))
- dx_section: bfloat16 [4096, 12288], P(('section', 'row', 'col'))
The draws below stay inside these ranges and needn't reach their ends.
Inputs may be any that keep to these rules, and one draw needn't show every extreme that they name: At each grid position the slots below blk_count name distinct block positions (blk_row, blk_col); the other slots name arbitrary positions. `blk_col`: see blk_row. `blk_count`: some grid position of every draw holds exactly 115 live slots. `tok_count`: index 0 counts the forward micro-batch, index 1 the backward one; valid tokens come first; some entry of every draw equals 256. `owner_order`: each section's row is a permutation.
All inputs are finite; a program needn't handle non-finite values.
Results may differ from the reference program's by a relative error of at most 0.015.
Values may be sent and summed in bfloat16 or wider, within the bound.
A program may use at most 128 MiB of HBM per device.

```python
import jax
import jax.numpy as jnp
from jax import lax

DMODEL = 12288
DIN = 12288
BLK = 128
TOK = 256
NBI = 96
NBO = 96
BR = 12
BC = 24
POS = 288
CAP = 115
NRB = 64
RB = 4
TOKENS = 4096
N_SECTION = 16
N_ROW = 8
N_COL = 4


def pattern_lists(key):
    key_count, key_pick, key_order = jax.random.split(jax.random.fold_in(key, 7), 3)
    grid_shape = (N_SECTION, N_ROW, N_COL)
    device_total = N_SECTION * N_ROW * N_COL
    counts = jax.random.randint(key_count, grid_shape, POS // 5, 2 * POS // 5 + 1)
    chosen = jax.random.randint(key_pick, (), 0, device_total)
    position = jnp.arange(device_total).reshape(grid_shape)
    counts = jnp.where(position == chosen, CAP, counts).astype(jnp.int32)
    scores = jax.random.randint(key_order, grid_shape + (POS,), 0, 2 ** 20) * POS + jnp.arange(POS)
    shuffled = jnp.argsort(scores, axis=-1)[..., :CAP].astype(jnp.int32)
    return (counts, (shuffled // BC).astype(jnp.int32), (shuffled % BC).astype(jnp.int32))


def draw_blk_row(key, part):
    return pattern_lists(key)[1]


def draw_blk_col(key, part):
    return pattern_lists(key)[2]


def draw_blk_count(key, part):
    return pattern_lists(key)[0]


def draw_tok_count(key, part):
    key_count, key_pick = jax.random.split(jax.random.fold_in(key, 11), 2)
    counts = jax.random.randint(key_count, (N_SECTION, 2), TOK // 4, TOK + 1)
    chosen = jax.random.randint(key_pick, (), 0, 2 * N_SECTION)
    position = jnp.arange(2 * N_SECTION).reshape(N_SECTION, 2)
    return jnp.where(position == chosen, TOK, counts).astype(jnp.int32)


def shard_levels(own_key, extent, pieces, smallest, top_value):
    loudness = 1.0
    for axis_at, parts in pieces:
        draws = jax.random.uniform(jax.random.fold_in(jax.random.fold_in(own_key, 6), axis_at), (parts,), jnp.float32, smallest / len(pieces), top_value / len(pieces))
        loudness = loudness * jnp.repeat(jnp.exp(draws), extent[axis_at] // parts).reshape((-1,) + (1,) * (len(extent) - 1 - axis_at))
    return loudness


def centred(own_key, shape, deviation, bound, shards=(), dtype=jnp.bfloat16):
    entries = jax.random.normal(own_key, shape, jnp.float32) * deviation
    if len(shards) > 0:
        entries = shard_levels(own_key, shape, shards, -0.22, 0.18) * entries
    return jnp.clip(entries, min=-bound, max=bound).astype(dtype)


def setup_inputs(seed: int = 0) -> dict:
    key_of = jax.random.split(jax.random.key(seed), 9)
    return {
        "x_fwd": centred(key_of[0], (TOKENS, DIN), 1.0, 6.0, ((0, 16), (1, 8))),
        "dy_bwd": centred(key_of[1], (TOKENS, DMODEL), 1.0, 6.0, ((0, 128), (1, 4))),
        "w_blocks": centred(key_of[2], (N_SECTION, N_ROW, N_COL, CAP, BLK, BLK), (3 * DIN // 10) ** -0.5, 0.09375, ((0, 16), (1, 8), (2, 4))),
        "blk_row": draw_blk_row(jax.random.fold_in(key_of[8], 71), 0),
        "blk_col": draw_blk_col(jax.random.fold_in(key_of[8], 71), 0),
        "blk_count": draw_blk_count(jax.random.fold_in(key_of[8], 71), 0),
        "tok_count": draw_tok_count(jax.random.fold_in(key_of[8], 71), 0),
        "owner_order": jax.vmap(lambda own: jax.random.permutation(own, NRB))(jax.random.split(key_of[7], N_SECTION)).reshape((N_SECTION, NRB)).astype(jnp.int32),
    }


def section_pass(inputs):
    x_section, dy_section, w_section, row_slots, col_slots, live_count, tok_limit, owner_rows = inputs
    live = (jnp.arange(CAP)[None, None, :] < live_count[:, :, None]).astype(jnp.float32)
    global_rows = jnp.arange(N_ROW)[:, None, None] * BR + row_slots
    global_cols = jnp.arange(N_COL)[None, :, None] * BC + col_slots
    w_live = w_section.astype(jnp.float32) * live[:, :, :, None, None]
    positions = jnp.arange(TOK)
    keep_fwd = (positions < tok_limit[0]).astype(jnp.float32)
    keep_bwd = (positions < tok_limit[1]).astype(jnp.float32)

    x_blocks = (x_section.astype(jnp.float32) * keep_fwd[:, None]).reshape(TOK, NBI, BLK)
    x_slots = jnp.take(x_blocks, global_rows.reshape(-1), axis=1).reshape(TOK, N_ROW, N_COL * CAP, BLK)
    products = jnp.einsum("trkb,rkbc->trkc", x_slots, w_live.reshape(N_ROW, N_COL * CAP, BLK, BLK),
                          precision=lax.Precision.HIGHEST)
    row_index = jnp.arange(N_ROW)[:, None]
    partial_value = jnp.zeros((TOK, N_ROW, NBO, BLK), jnp.float32).at[
        :, row_index, global_cols.reshape(N_ROW, N_COL * CAP)].add(products)
    rounded = lax.optimization_barrier(partial_value.astype(jnp.bfloat16)).astype(jnp.float32)
    forward = jnp.sum(rounded, axis=1).reshape(TOK, DMODEL).astype(jnp.bfloat16)
    forward = forward.reshape(NRB, RB, DMODEL)[owner_rows].reshape(TOK, DMODEL)

    dy_blocks = (dy_section.astype(jnp.float32) * keep_bwd[:, None]).reshape(TOK, NBO, BLK)
    cols_by_col = jnp.transpose(global_cols, (1, 0, 2)).reshape(N_COL, N_ROW * CAP)
    rows_by_col = jnp.transpose(global_rows * jnp.ones_like(global_cols), (1, 0, 2)).reshape(N_COL, N_ROW * CAP)
    w_by_col = jnp.transpose(w_live, (1, 0, 2, 3, 4)).reshape(N_COL, N_ROW * CAP, BLK, BLK)
    dy_slots = jnp.take(dy_blocks, cols_by_col.reshape(-1), axis=1).reshape(TOK, N_COL, N_ROW * CAP, BLK)
    back_products = jnp.einsum("tckn,ckmn->tckm", dy_slots, w_by_col, precision=lax.Precision.HIGHEST)
    col_index = jnp.arange(N_COL)[:, None]
    back_partial = jnp.zeros((TOK, N_COL, NBI, BLK), jnp.float32).at[
        :, col_index, rows_by_col].add(back_products)
    back_rounded = lax.optimization_barrier(back_partial.astype(jnp.bfloat16)).astype(jnp.float32)
    backward = jnp.sum(back_rounded, axis=1).reshape(TOK, DIN).astype(jnp.bfloat16)
    return forward, backward


def reference(x_fwd, dy_bwd, w_blocks, blk_row, blk_col, blk_count, tok_count, owner_order):
    stacked = (x_fwd.reshape(N_SECTION, TOK, DIN), dy_bwd.reshape(N_SECTION, TOK, DMODEL), w_blocks,
               blk_row, blk_col, blk_count, tok_count, owner_order)
    forward, backward = lax.map(section_pass, stacked)
    shifted = jnp.concatenate([jnp.zeros((1, TOK, DMODEL), jnp.bfloat16), forward[:-1]], axis=0)
    return shifted.reshape(TOKENS, DMODEL), backward.reshape(TOKENS, DIN)
```

```python
import functools

import jax
import jax.numpy as jnp
from jax import lax
from jax.experimental import pallas as pl
from jax.experimental.pallas import tpu as pltpu
from jax.sharding import PartitionSpec as P

MESH = pl.DeviceIdType.MESH
F32 = jnp.float32
BF16 = jnp.bfloat16
FWD_UNITS = 4
BWD_UNITS = 2


def kernel(
    sizes,
    slot_ref,
    tok_ref,
    owner_ref,
    x_hbm,
    dy_hbm,
    w_hbm,
    y_out,
    dx_out,
    w,
    x,
    xp,
    dy_all,
    part,
    pair_in,
    summed,
    fwd_relay,
    fwd_direct,
    fwd_comb,
    fwd_fin,
    bpart,
    bwd_relay,
    bwd_direct,
    bwd_comb,
    bwd_fin,
    load_sem,
    gather_send,
    gather_recv,
    pair_send,
    pair_recv,
    fring_send,
    fring_recv,
    ffin_send,
    y_recv,
    bring_send,
    bring_recv,
    bfin_send,
    dx_recv,
):
    sections, rows, cols, block_rows, block_cols = sizes
    blk = w.shape[1]
    slot_total = w_hbm.shape[0]
    tokens, in_width = x.shape
    out_width = dy_all.shape[2]
    shard = dy_all.shape[1]
    fwd_width = out_width // FWD_UNITS
    bwd_width = in_width // BWD_UNITS

    sec = lax.axis_index("section")
    row = lax.axis_index("row")
    col = lax.axis_index("col")
    height, core = row // 2, row % 2
    ring = rows // 2
    later_sec = lax.rem(sec + 1, sections)
    earlier_sec = lax.rem(sec + sections - 1, sections)

    def high(by):
        return lax.rem(height + by + ring, ring)

    def across(by):
        return lax.rem(col + by + cols, cols)

    sibling = (sec, height * 2 + 1 - core, col)

    def tall(by):
        return (sec, high(by) * 2 + core, col)

    def wide(by):
        return (sec, row, across(by))

    load_w = pltpu.make_async_copy(w_hbm, w.at[pl.ds(0, slot_total)], load_sem.at[0])
    load_x = pltpu.make_async_copy(x_hbm, x, load_sem.at[1])
    load_dy = pltpu.make_async_copy(dy_hbm, dy_all.at[row], load_sem.at[2])
    load_dy.start()
    load_x.start()
    load_w.start()

    barrier = pltpu.get_barrier_semaphore()

    def greet(device):
        pl.semaphore_signal(barrier, inc=1, device_id=device, device_id_type=MESH)

    for by in range(1, rows):
        greet((sec, lax.rem(row + by, rows), col))
    greet(wide(1))
    greet(wide(-1))
    for c in range(cols):
        greet((later_sec, row, c))
        greet((earlier_sec, row, c))
    w[slot_total] = jnp.zeros((blk, blk), BF16)
    pl.semaphore_wait(barrier, rows + 1 + 2 * cols)

    def gather(k, src_row, lo, width, device):
        place = dy_all.at[src_row, :, pl.ds(lo, width)]
        return pltpu.make_async_remote_copy(
            src_ref=place,
            dst_ref=place,
            send_sem=gather_send.at[k],
            recv_sem=gather_recv.at[k],
            device_id=device,
            device_id_type=MESH,
        )

    half = out_width // 2
    below, above, far = high(-1) * 2 + core, high(1) * 2 + core, high(2) * 2 + core
    twin = 1 - 2 * core

    load_dy.wait()
    g_up = gather(0, row, 0, out_width, tall(1))
    g_down = gather(1, row, 0, out_width, tall(-1))
    g_own = gather(2, row, 0, out_width, sibling)
    g_up.start()
    g_down.start()
    g_own.start()

    limit = tok_ref[0, 0]
    blocks = owner_ref.shape[1]
    length = tokens // blocks
    half_rows = tokens // 2

    def delivered(m):
        k = m // half_rows
        rest = m % half_rows
        return ((rest // shard) * 2 + k) * shard + rest % shard

    place = delivered(lax.broadcasted_iota(jnp.int32, (blocks, tokens), 1)) // length
    spread = (place == lax.broadcasted_iota(jnp.int32, (blocks, tokens), 0)).astype(F32).astype(BF16)
    owners = jnp.broadcast_to(owner_ref[...].astype(F32), (8, blocks)).astype(BF16)
    owner_row = jnp.dot(owners, spread, preferred_element_type=F32)[0:1]
    inner = (lax.broadcasted_iota(jnp.int32, (1, tokens), 1) % length).astype(F32)
    source = owner_row * length + inner
    source = jnp.where(source < limit.astype(F32), source, -1.0)
    token = lax.broadcasted_iota(jnp.int32, (tokens, tokens), 0).astype(F32)
    pick = jnp.where(token == source, 1.0, 0.0).astype(F32).T.astype(BF16)
    load_x.wait()
    xp[...] = jnp.dot(pick, x[...], preferred_element_type=F32).astype(BF16)
    load_w.wait()

    def fwd_dot(u):
        def tile(n, carry):
            first = (u * (fwd_width // (2 * blk)) + n) * 2
            rhs = jnp.concatenate(
                [
                    jnp.concatenate(
                        [w[slot_ref[r * block_cols + first + j]] for j in range(2)], axis=1
                    )
                    for r in range(block_rows)
                ],
                axis=0,
            )
            out = jnp.dot(xp[...], rhs, preferred_element_type=F32)
            at = pl.ds(pl.multiple_of(n * 2 * blk, 2 * blk), 2 * blk)
            part[u, :, :, at] = out.astype(BF16).reshape(2, half_rows, 2 * blk)
            return carry

        lax.fori_loop(0, fwd_width // (2 * blk), tile, 0)

    def pair_copy(u):
        return pltpu.make_async_remote_copy(
            src_ref=part.at[u, 1 - core],
            dst_ref=pair_in.at[u],
            send_sem=pair_send.at[u],
            recv_sem=pair_recv.at[u],
            device_id=sibling,
            device_id_type=MESH,
        )

    def fwd_ring(u, k):
        way = 1 if u % 2 == 0 else -1
        by, dst, to = ((2, fwd_relay, way), (-way, fwd_direct, -way), (way, fwd_comb, way))[k]
        return pltpu.make_async_remote_copy(
            src_ref=summed.at[u, high(by)],
            dst_ref=dst.at[u],
            send_sem=fring_send.at[u, k],
            recv_sem=fring_recv.at[u, k],
            device_id=tall(to),
            device_id_type=MESH,
        )

    def fwd_pair(u):
        pair_copy(u).wait_recv()
        both = part[u, core].astype(F32) + pair_in[u].astype(F32)
        summed[u] = both.astype(BF16).reshape(ring, shard, fwd_width)
        fwd_ring(u, 0).start()
        fwd_ring(u, 1).start()

    def fwd_mid(u):
        way = 1 if u % 2 == 0 else -1
        fwd_ring(u, 0).wait_recv()
        there = high(way)
        summed[u, there] = (summed[u, there].astype(F32) + fwd_relay[u].astype(F32)).astype(BF16)
        fwd_ring(u, 2).start()

    def y_copy(u, c):
        return pltpu.make_async_remote_copy(
            src_ref=fwd_fin.at[u, c],
            dst_ref=y_out.at[:, pl.ds(pl.multiple_of(col * out_width + u * fwd_width, 128), fwd_width)],
            send_sem=ffin_send.at[u, c],
            recv_sem=y_recv,
            device_id=(later_sec, row, c),
            device_id_type=MESH,
        )

    def fwd_end(u):
        fwd_ring(u, 1).wait_recv()
        fwd_ring(u, 2).wait_recv()
        total = summed[u, height].astype(F32) + fwd_direct[u].astype(F32) + fwd_comb[u].astype(F32)
        fwd_fin[u] = total.reshape(cols, shard // cols, fwd_width).astype(BF16)
        for c in range(cols):
            y_copy(u, c).start()

    def bwd_dot(v):
        def tile(n, carry):
            first = (v * (bwd_width // (2 * blk)) + n) * 2
            rhs = jnp.concatenate(
                [
                    jnp.concatenate(
                        [w[slot_ref[(first + j) * block_cols + c]] for j in range(2)], axis=0
                    )
                    for c in range(block_cols)
                ],
                axis=1,
            )
            out = lax.dot_general(
                dy_all[...].reshape(tokens, out_width),
                rhs,
                (((1,), (1,)), ((), ())),
                preferred_element_type=F32,
            )
            at = pl.ds(pl.multiple_of(n * 2 * blk, 2 * blk), 2 * blk)
            bpart[v, :, :, :, at] = out.reshape(rows, cols, shard // cols, 2 * blk).astype(BF16)
            return carry

        lax.fori_loop(0, bwd_width // (2 * blk), tile, 0)

    def bwd_ring(v, k):
        way = 1 if v % 2 == 0 else -1
        by, dst, to = ((2, bwd_relay, way), (-way, bwd_direct, -way), (way, bwd_comb, way))[k]
        return pltpu.make_async_remote_copy(
            src_ref=bpart.at[v, :, across(by)],
            dst_ref=dst.at[v],
            send_sem=bring_send.at[v, k],
            recv_sem=bring_recv.at[v, k],
            device_id=wide(to),
            device_id_type=MESH,
        )

    def bwd_mid(v):
        way = 1 if v % 2 == 0 else -1
        bwd_ring(v, 0).wait_recv()
        there = across(way)
        bpart[v, :, there] = (bpart[v, :, there].astype(F32) + bwd_relay[v].astype(F32)).astype(BF16)
        bwd_ring(v, 2).start()

    def dx_at(v):
        return dx_out.at[:, pl.ds(pl.multiple_of(row * in_width + v * bwd_width, 128), bwd_width)]

    def dx_copy(v, by):
        to = lax.rem(row + by, rows)
        return pltpu.make_async_remote_copy(
            src_ref=bwd_fin.at[v, to],
            dst_ref=dx_at(v),
            send_sem=bfin_send.at[v, by],
            recv_sem=dx_recv,
            device_id=(sec, to, col),
            device_id_type=MESH,
        )

    def dx_own(v):
        return pltpu.make_async_copy(bwd_fin.at[v, row], dx_at(v), bfin_send.at[v, 0])

    def bwd_end(v):
        bwd_ring(v, 1).wait_recv()
        bwd_ring(v, 2).wait_recv()
        total = bpart[v, :, col].astype(F32) + bwd_direct[v].astype(F32) + bwd_comb[v].astype(F32)
        bwd_fin[v] = total.astype(BF16)
        for by in range(1, rows):
            dx_copy(v, by).start()
        dx_own(v).start()

    fwd_dot(0)
    pair_copy(0).start()
    fwd_dot(1)
    pair_copy(1).start()
    fwd_pair(0)

    gather(0, below, 0, out_width, tall(1)).wait_recv()
    g_on_up = gather(3, below, 0, half, tall(1))
    g_on_up.start()
    g_below = gather(5, below, 0, out_width, sibling)
    g_below.start()
    gather(1, above, 0, out_width, tall(-1)).wait_recv()
    g_on_down = gather(4, above, half, half, tall(-1))
    g_on_down.start()
    g_above = gather(6, above, 0, out_width, sibling)
    g_above.start()

    fwd_dot(2)
    pair_copy(2).start()
    fwd_pair(1)
    fwd_dot(3)
    pair_copy(3).start()
    fwd_pair(2)
    gather(3, far, 0, half, tall(1)).wait_recv()
    g_far_low = gather(7, far, 0, half, sibling)
    g_far_low.start()
    gather(4, far, half, half, tall(-1)).wait_recv()
    g_far_high = gather(8, far, half, half, sibling)
    g_far_high.start()
    fwd_pair(3)
    fwd_mid(0)
    fwd_mid(1)

    gather(2, row + twin, 0, out_width, sibling).wait_recv()
    gather(5, below + twin, 0, out_width, sibling).wait_recv()
    gather(6, above + twin, 0, out_width, sibling).wait_recv()
    gather(7, far + twin, 0, half, sibling).wait_recv()
    gather(8, far + twin, half, half, sibling).wait_recv()

    bwd_dot(0)
    bwd_ring(0, 0).start()
    bwd_ring(0, 1).start()
    fwd_mid(2)
    fwd_mid(3)
    fwd_end(0)
    fwd_end(1)
    bwd_dot(1)
    bwd_ring(1, 0).start()
    bwd_ring(1, 1).start()
    bwd_mid(0)
    fwd_end(2)
    fwd_end(3)
    bwd_mid(1)
    bwd_end(0)
    bwd_end(1)

    for copy in (g_up, g_down, g_own, g_on_up, g_on_down, g_below, g_above, g_far_low, g_far_high):
        copy.wait_send()
    for u in range(FWD_UNITS):
        pair_copy(u).wait_send()
        for k in range(3):
            fwd_ring(u, k).wait_send()
        for c in range(cols):
            y_copy(u, c).wait_send()
    for v in range(BWD_UNITS):
        for k in range(3):
            bwd_ring(v, k).wait_send()
        for by in range(1, rows):
            dx_copy(v, by).wait_send()
        dx_own(v).wait()

    pltpu.make_async_remote_copy(
        src_ref=y_out,
        dst_ref=y_out,
        send_sem=y_recv,
        recv_sem=y_recv,
        device_id=sibling,
        device_id_type=MESH,
    ).wait_recv()
    others = dx_out.at[:, pl.ds(0, (rows - 1) * in_width)]
    pltpu.make_async_remote_copy(
        src_ref=others,
        dst_ref=others,
        send_sem=dx_recv,
        recv_sem=dx_recv,
        device_id=sibling,
        device_id_type=MESH,
    ).wait_recv()


def local(x_fwd, dy_bwd, w_blocks, blk_row, blk_col, blk_count, tok_count, owner_order):
    sections = lax.axis_size("section")
    rows = lax.axis_size("row")
    cols = lax.axis_size("col")
    ring = rows // 2
    tokens, in_width = x_fwd.shape
    shard, out_width = dy_bwd.shape
    slot_total = w_blocks.shape[3]
    blk = w_blocks.shape[5]
    block_rows, block_cols = in_width // blk, out_width // blk
    positions = block_rows * block_cols
    owned = tokens // (rows * cols)
    fwd_width = out_width // FWD_UNITS
    bwd_width = in_width // BWD_UNITS

    slots = jnp.arange(slot_total)
    where_to = blk_row.reshape(slot_total) * block_cols + blk_col.reshape(slot_total)
    where_to = jnp.where(slots < blk_count.reshape(()), where_to, -1)
    slot_of = jnp.min(
        jnp.where(where_to[None, :] == jnp.arange(positions)[:, None], slots[None, :], slot_total), axis=1
    ).astype(jnp.int32)

    dma = pltpu.SemaphoreType.DMA
    y_raw, dx_raw = pl.pallas_call(
        functools.partial(kernel, (sections, rows, cols, block_rows, block_cols)),
        out_shape=(
            jax.ShapeDtypeStruct((owned, cols * out_width), BF16),
            jax.ShapeDtypeStruct((owned, rows * in_width), BF16),
        ),
        in_specs=[
            pl.BlockSpec(memory_space=pltpu.SMEM),
            pl.BlockSpec(memory_space=pltpu.SMEM),
            pl.BlockSpec(memory_space=pltpu.VMEM),
            pl.BlockSpec(memory_space=pl.ANY),
            pl.BlockSpec(memory_space=pl.ANY),
            pl.BlockSpec(memory_space=pl.ANY),
        ],
        out_specs=(pl.BlockSpec(memory_space=pl.ANY), pl.BlockSpec(memory_space=pl.ANY)),
        scratch_shapes=[
            pltpu.VMEM((slot_total + 1, blk, blk), BF16),
            pltpu.VMEM((tokens, in_width), BF16),
            pltpu.VMEM((tokens, in_width), BF16),
            pltpu.VMEM((rows, shard, out_width), BF16),
            pltpu.VMEM((FWD_UNITS, 2, tokens // 2, fwd_width), BF16),
            pltpu.VMEM((FWD_UNITS, tokens // 2, fwd_width), BF16),
            pltpu.VMEM((FWD_UNITS, ring, shard, fwd_width), BF16),
            pltpu.VMEM((FWD_UNITS, shard, fwd_width), BF16),
            pltpu.VMEM((FWD_UNITS, shard, fwd_width), BF16),
            pltpu.VMEM((FWD_UNITS, shard, fwd_width), BF16),
            pltpu.VMEM((FWD_UNITS, cols, owned, fwd_width), BF16),
            pltpu.VMEM((BWD_UNITS, rows, cols, owned, bwd_width), BF16),
            pltpu.VMEM((BWD_UNITS, rows, owned, bwd_width), BF16),
            pltpu.VMEM((BWD_UNITS, rows, owned, bwd_width), BF16),
            pltpu.VMEM((BWD_UNITS, rows, owned, bwd_width), BF16),
            pltpu.VMEM((BWD_UNITS, rows, owned, bwd_width), BF16),
            dma((3,)),
            dma((9,)),
            dma((9,)),
            dma((FWD_UNITS,)),
            dma((FWD_UNITS,)),
            dma((FWD_UNITS, 3)),
            dma((FWD_UNITS, 3)),
            dma((FWD_UNITS, cols)),
            dma,
            dma((BWD_UNITS, 3)),
            dma((BWD_UNITS, 3)),
            dma((BWD_UNITS, rows)),
            dma,
        ],
        compiler_params=pltpu.CompilerParams(
            collective_id=0, has_side_effects=True, vmem_limit_bytes=40 * 1024 * 1024
        ),
    )(
        slot_of,
        tok_count,
        owner_order,
        x_fwd,
        dy_bwd,
        w_blocks.reshape(slot_total, blk, blk),
    )
    y_next = jnp.where(lax.axis_index("section") == 0, jnp.zeros_like(y_raw), y_raw)
    owner = (lax.axis_index("row") * cols + lax.axis_index("col")) * owned
    token = owner + lax.broadcasted_iota(jnp.int32, dx_raw.shape, 0)
    dx_section = jnp.where(token < tok_count[0, 1], dx_raw, jnp.zeros_like(dx_raw))
    return (y_next, dx_section)


def solution(mesh):
    return jax.shard_map(
        local,
        mesh=mesh,
        in_specs=(
            P("section", "row"),
            P(("section", "row"), "col"),
            P("section", "row", "col", None, None, None),
            P("section", "row", "col", None),
            P("section", "row", "col", None),
            P("section", "row", "col"),
            P("section", None),
            P("section", None),
        ),
        out_specs=(P(("section", "row", "col"), None), P(("section", "row", "col"), None)),
        check_vma=False,
    )
```

```python
import functools

import jax
import jax.numpy as jnp
from jax import lax
from jax.experimental import pallas as pl
from jax.experimental.pallas import tpu as pltpu
from jax.sharding import PartitionSpec as P

MESH = pl.DeviceIdType.MESH
F32 = jnp.float32
BF16 = jnp.bfloat16
FWD_UNITS = 6
BWD_UNITS = 6
BWD_GROUP = 2


def kernel(
    sizes,
    count_ref,
    tok_hbm,
    owner_hbm,
    blk_row_hbm,
    blk_col_hbm,
    x_hbm,
    dy_hbm,
    w_hbm,
    y_out,
    dx_out,
    tok_ref,
    owner_ref,
    blk_row_ref,
    blk_col_ref,
    slot_ref,
    slot_row,
    w,
    x,
    xp,
    dy_all,
    part,
    pair_in,
    summed,
    fwd_relay,
    fwd_direct,
    fwd_comb,
    fwd_fin,
    bpart,
    bwd_relay,
    bwd_direct,
    bwd_comb,
    bwd_fin,
    load_sem,
    gather_send,
    gather_recv,
    pair_send,
    pair_recv,
    fring_send,
    fring_recv,
    ffin_send,
    y_recv,
    bring_send,
    bring_recv,
    bfin_send,
    dx_recv,
):
    sections, rows, cols, block_rows, block_cols = sizes
    blk = w.shape[1]
    slot_total = w_hbm.shape[0]
    tokens, in_width = x.shape
    out_width = dy_all.shape[2]
    shard = dy_all.shape[1]
    fwd_width = out_width // FWD_UNITS
    bwd_width = in_width // BWD_UNITS

    sec = lax.axis_index("section")
    row = lax.axis_index("row")
    col = lax.axis_index("col")
    height, core = row // 2, row % 2
    ring = rows // 2

    def high(by):
        return lax.rem(height + by + ring, ring)

    def across(by):
        return lax.rem(col + by + cols, cols)

    sibling = (sec, height * 2 + 1 - core, col)

    def tall(by):
        return (sec, high(by) * 2 + core, col)

    def wide(by):
        return (sec, row, across(by))

    load_w = pltpu.make_async_copy(w_hbm, w.at[pl.ds(0, slot_total)], load_sem.at[0])
    load_x = pltpu.make_async_copy(x_hbm, x, load_sem.at[1])
    load_dy = pltpu.make_async_copy(dy_hbm, dy_all.at[row], load_sem.at[2])
    load_dy.start()
    small = [
        pltpu.make_async_copy(there, here, load_sem.at[4 + k])
        for k, (there, here) in enumerate(
            (
                (blk_row_hbm, blk_row_ref),
                (blk_col_hbm, blk_col_ref),
                (tok_hbm, tok_ref),
                (owner_hbm, owner_ref),
            )
        )
    ]
    for copy in small:
        copy.start()
    load_x.start()
    load_w.start()

    barrier = pltpu.get_barrier_semaphore()

    def greet(device):
        pl.semaphore_signal(barrier, inc=1, device_id=device, device_id_type=MESH)

    for by in range(1, rows):
        greet((sec, lax.rem(row + by, rows), col))
    greet(wide(1))
    greet(wide(-1))

    @pl.when(sec > 0)
    def _():
        for c in range(cols):
            greet((sec - 1, row, c))


    @pl.when(sec < sections - 1)
    def _():
        pl.semaphore_wait(barrier, rows + 1 + cols)

    @pl.when(sec == sections - 1)
    def _():
        pl.semaphore_wait(barrier, rows + 1)

    def gather(k, src_row, lo, width, device):
        place = dy_all.at[src_row, :, pl.ds(lo, width)]
        return pltpu.make_async_remote_copy(
            src_ref=place,
            dst_ref=place,
            send_sem=gather_send.at[k],
            recv_sem=gather_recv.at[k],
            device_id=device,
            device_id_type=MESH,
        )

    half = out_width // 2
    below, above, far = high(-1) * 2 + core, high(1) * 2 + core, high(2) * 2 + core
    twin = 1 - 2 * core

    load_dy.wait()
    gathers = [
        gather(0, row, 0, half, tall(1)),
        gather(1, row, half, half, tall(-1)),
        gather(2, row, half, half, tall(1)),
        gather(3, row, 0, half, tall(-1)),
        gather(4, row, 0, out_width, sibling),
    ]
    for copy in gathers:
        copy.start()

    def hand_on(*copies):
        for copy in copies:
            copy.start()
            gathers.append(copy)

    for copy in small:
        copy.wait()
    w[slot_total] = jnp.zeros((blk, blk), BF16)

    slot = lax.broadcasted_iota(jnp.int32, (1, slot_total), 1)
    target = blk_row_ref[...] * block_cols + blk_col_ref[...]
    target = jnp.where(slot < count_ref[0, 0, 0], target, -1)
    target = jnp.concatenate([target, jnp.full((1, blk - slot_total), -1, jnp.int32)], axis=1)
    target = jnp.broadcast_to(target, (8, blk)).T[:, 0:1]
    held = jnp.where(
        target == lax.broadcasted_iota(jnp.int32, (blk, slot_row.shape[1]), 1),
        lax.broadcasted_iota(jnp.int32, (blk, slot_row.shape[1]), 0),
        slot_total,
    )
    slot_row[...] = jnp.min(held, axis=0, keepdims=True)
    load_slots = pltpu.make_async_copy(slot_row, slot_ref, load_sem.at[3])
    load_slots.start()
    limit = tok_ref[0, 0]
    blocks = owner_ref.shape[1]
    length = tokens // blocks
    half_rows = tokens // 2

    def delivered(m):
        k = m // half_rows
        rest = m % half_rows
        return ((rest // shard) * 2 + k) * shard + rest % shard

    place = delivered(lax.broadcasted_iota(jnp.int32, (blocks, tokens), 1)) // length
    spread = (place == lax.broadcasted_iota(jnp.int32, (blocks, tokens), 0)).astype(F32).astype(BF16)
    owners = jnp.broadcast_to(owner_ref[...].astype(F32), (8, blocks)).astype(BF16)
    owner_row = jnp.dot(owners, spread, preferred_element_type=F32)[0:1]
    inner = (lax.broadcasted_iota(jnp.int32, (1, tokens), 1) % length).astype(F32)
    source = owner_row * length + inner
    source = jnp.where(source < limit.astype(F32), source, -1.0)
    token = lax.broadcasted_iota(jnp.int32, (tokens, tokens), 0).astype(F32)
    pick = jnp.where(token == source, 1.0, 0.0).astype(F32).T.astype(BF16)
    load_x.wait()
    xp[...] = jnp.dot(pick, x[...], preferred_element_type=F32).astype(BF16)
    load_slots.wait()
    load_w.wait()

    def fwd_dot(u):
        def tile(n, carry):
            first = (u * (fwd_width // (2 * blk)) + n) * 2
            rhs = jnp.concatenate(
                [
                    jnp.concatenate(
                        [w[slot_ref[0, r * block_cols + first + j]] for j in range(2)], axis=1
                    )
                    for r in range(block_rows)
                ],
                axis=0,
            )
            out = jnp.dot(xp[...], rhs, preferred_element_type=F32)
            at = pl.ds(pl.multiple_of(n * 2 * blk, 2 * blk), 2 * blk)
            part[u, :, :, at] = out.astype(BF16).reshape(2, half_rows, 2 * blk)
            return carry

        lax.fori_loop(0, fwd_width // (2 * blk), tile, 0)

    def pair_copy(u):
        return pltpu.make_async_remote_copy(
            src_ref=part.at[u, 1 - core],
            dst_ref=pair_in.at[u],
            send_sem=pair_send.at[u],
            recv_sem=pair_recv.at[u],
            device_id=sibling,
            device_id_type=MESH,
        )

    def fwd_ring(u, k):
        way = 1 if u % 2 == 0 else -1
        by, dst, to = ((2, fwd_relay, way), (-way, fwd_direct, -way), (way, fwd_comb, way))[k]
        return pltpu.make_async_remote_copy(
            src_ref=summed.at[u, high(by)],
            dst_ref=dst.at[u],
            send_sem=fring_send.at[u, k],
            recv_sem=fring_recv.at[u, k],
            device_id=tall(to),
            device_id_type=MESH,
        )

    def fwd_pair(u):
        pair_copy(u).wait_recv()
        both = part[u, core].astype(F32) + pair_in[u].astype(F32)
        summed[u] = both.astype(BF16).reshape(ring, shard, fwd_width)
        fwd_ring(u, 0).start()
        fwd_ring(u, 1).start()

    def fwd_mid(u):
        way = 1 if u % 2 == 0 else -1
        fwd_ring(u, 0).wait_recv()
        there = high(way)
        summed[u, there] = (summed[u, there].astype(F32) + fwd_relay[u].astype(F32)).astype(BF16)
        fwd_ring(u, 2).start()

    def y_copy(u, c):
        return pltpu.make_async_remote_copy(
            src_ref=fwd_fin.at[u, c],
            dst_ref=y_out.at[:, pl.ds(pl.multiple_of(col * out_width + u * fwd_width, 128), fwd_width)],
            send_sem=ffin_send.at[u, c],
            recv_sem=y_recv,
            device_id=(sec + 1, row, c),
            device_id_type=MESH,
        )

    def fwd_end(u):
        fwd_ring(u, 1).wait_recv()
        fwd_ring(u, 2).wait_recv()
        total = summed[u, height].astype(F32) + fwd_direct[u].astype(F32) + fwd_comb[u].astype(F32)
        fwd_fin[u] = total.reshape(cols, shard // cols, fwd_width).astype(BF16)

        @pl.when(sec < sections - 1)
        def _():
            for c in range(cols):
                y_copy(u, c).start()

    def bwd_dot(v):
        def tile(n, carry):
            first = (v * (bwd_width // (2 * blk)) + n) * 2
            rhs = jnp.concatenate(
                [
                    jnp.concatenate(
                        [w[slot_ref[0, (first + j) * block_cols + c]] for j in range(2)], axis=0
                    )
                    for c in range(block_cols)
                ],
                axis=1,
            )
            out = lax.dot_general(
                dy_all[...].reshape(tokens, out_width),
                rhs,
                (((1,), (1,)), ((), ())),
                preferred_element_type=F32,
            )
            at = pl.ds(pl.multiple_of(n * 2 * blk, 2 * blk), 2 * blk)
            out = out.reshape(rows, cols, shard // cols, 2 * blk).astype(BF16)
            for c in range(cols):
                bpart[v, c, :, :, at] = out[:, c]
            return carry

        lax.fori_loop(0, bwd_width // (2 * blk), tile, 0)

    def bwd_ring(v, k):
        way = 1 if v % 2 == 0 else -1
        by, dst, to = ((2, bwd_relay, way), (-way, bwd_direct, -way), (way, bwd_comb, way))[k]
        return pltpu.make_async_remote_copy(
            src_ref=bpart.at[v, across(by)],
            dst_ref=dst.at[v],
            send_sem=bring_send.at[v, k],
            recv_sem=bring_recv.at[v, k],
            device_id=wide(to),
            device_id_type=MESH,
        )

    def bwd_mid(v):
        way = 1 if v % 2 == 0 else -1
        bwd_ring(v, 0).wait_recv()
        there = across(way)
        bpart[v, there] = (bpart[v, there].astype(F32) + bwd_relay[v].astype(F32)).astype(BF16)
        bwd_ring(v, 2).start()

    group_width = BWD_GROUP * bwd_width

    def dx_at(g):
        return dx_out.at[:, pl.ds(pl.multiple_of(row * in_width + g * group_width, 128), group_width)]

    def dx_copy(g, by):
        to = lax.rem(row + by, rows)
        return pltpu.make_async_remote_copy(
            src_ref=bwd_fin.at[g, to],
            dst_ref=dx_at(g),
            send_sem=bfin_send.at[g, by],
            recv_sem=dx_recv,
            device_id=(sec, to, col),
            device_id_type=MESH,
        )

    def dx_own(g):
        return pltpu.make_async_copy(bwd_fin.at[g, row], dx_at(g), bfin_send.at[g, 0])

    def bwd_end(v):
        bwd_ring(v, 1).wait_recv()
        bwd_ring(v, 2).wait_recv()
        total = bpart[v, col].astype(F32) + bwd_direct[v].astype(F32) + bwd_comb[v].astype(F32)
        token = lax.broadcasted_iota(jnp.int32, total.shape, 0) * shard + col * (shard // cols)
        token = token + lax.broadcasted_iota(jnp.int32, total.shape, 1)
        total = jnp.where(token < tok_ref[0, 1], total, 0.0).astype(BF16)
        g = v // BWD_GROUP
        bwd_fin[g, :, :, pl.ds((v % BWD_GROUP) * bwd_width, bwd_width)] = total
        if v % BWD_GROUP == BWD_GROUP - 1:
            for by in range(1, rows):
                dx_copy(g, by).start()
            dx_own(g).start()

    def fwd_first(u):
        fwd_dot(u)
        pair_copy(u).start()

    def bwd_first(v):
        bwd_dot(v)
        bwd_ring(v, 0).start()
        bwd_ring(v, 1).start()

    fwd_first(0)
    fwd_first(1)
    fwd_first(2)
    fwd_first(3)
    gather(0, below, 0, half, tall(1)).wait_recv()
    hand_on(gather(5, below, 0, half, tall(1)), gather(6, below, 0, half, sibling))
    gather(1, above, half, half, tall(-1)).wait_recv()
    hand_on(gather(7, above, half, half, tall(-1)), gather(8, above, half, half, sibling))
    fwd_pair(0)
    fwd_pair(1)
    fwd_first(4)
    fwd_pair(2)
    fwd_first(5)
    gather(2, below, half, half, tall(1)).wait_recv()
    hand_on(gather(9, below, half, half, sibling))
    gather(3, above, 0, half, tall(-1)).wait_recv()
    hand_on(gather(10, above, 0, half, sibling))
    fwd_pair(3)
    fwd_pair(4)
    fwd_pair(5)
    gather(5, far, 0, half, tall(1)).wait_recv()
    hand_on(gather(11, far, 0, half, sibling))
    gather(7, far, half, half, tall(-1)).wait_recv()
    hand_on(gather(12, far, half, half, sibling))
    fwd_mid(0)
    fwd_mid(1)
    gather(4, row + twin, 0, out_width, sibling).wait_recv()
    gather(6, below + twin, 0, half, sibling).wait_recv()
    gather(8, above + twin, half, half, sibling).wait_recv()
    gather(9, below + twin, half, half, sibling).wait_recv()
    gather(10, above + twin, 0, half, sibling).wait_recv()
    gather(11, far + twin, 0, half, sibling).wait_recv()
    gather(12, far + twin, half, half, sibling).wait_recv()
    bwd_first(0)
    fwd_mid(2)
    bwd_first(1)
    fwd_mid(3)
    bwd_first(2)
    fwd_mid(4)
    bwd_first(3)
    bwd_first(4)
    fwd_mid(5)
    bwd_first(5)
    bwd_mid(0)
    fwd_end(0)
    fwd_end(1)
    fwd_end(2)
    bwd_mid(1)
    fwd_end(3)
    fwd_end(4)
    bwd_mid(2)
    bwd_mid(3)
    fwd_end(5)
    bwd_mid(4)
    bwd_mid(5)
    bwd_end(0)
    bwd_end(1)
    bwd_end(2)
    bwd_end(3)
    bwd_end(4)
    bwd_end(5)

    for copy in gathers:
        copy.wait_send()
    for u in range(FWD_UNITS):
        pair_copy(u).wait_send()
        for k in range(3):
            fwd_ring(u, k).wait_send()
    for v in range(BWD_UNITS):
        for k in range(3):
            bwd_ring(v, k).wait_send()
    for g in range(BWD_UNITS // BWD_GROUP):
        for by in range(1, rows):
            dx_copy(g, by).wait_send()
        dx_own(g).wait()

    @pl.when(sec < sections - 1)
    def _():
        for u in range(FWD_UNITS):
            for c in range(cols):
                y_copy(u, c).wait_send()

    @pl.when(sec > 0)
    def _():
        pltpu.make_async_remote_copy(
            src_ref=y_out,
            dst_ref=y_out,
            send_sem=y_recv,
            recv_sem=y_recv,
            device_id=sibling,
            device_id_type=MESH,
        ).wait_recv()

    others = dx_out.at[:, pl.ds(0, (rows - 1) * in_width)]
    pltpu.make_async_remote_copy(
        src_ref=others,
        dst_ref=others,
        send_sem=dx_recv,
        recv_sem=dx_recv,
        device_id=sibling,
        device_id_type=MESH,
    ).wait_recv()


def local(x_fwd, dy_bwd, w_blocks, blk_row, blk_col, blk_count, tok_count, owner_order):
    sections = lax.axis_size("section")
    rows = lax.axis_size("row")
    cols = lax.axis_size("col")
    ring = rows // 2
    tokens, in_width = x_fwd.shape
    shard, out_width = dy_bwd.shape
    slot_total = w_blocks.shape[3]
    blk = w_blocks.shape[5]
    block_rows, block_cols = in_width // blk, out_width // blk
    table = pl.cdiv(block_rows * block_cols, 128) * 128
    owned = tokens // (rows * cols)
    fwd_width = out_width // FWD_UNITS
    bwd_width = in_width // BWD_UNITS

    dma = pltpu.SemaphoreType.DMA
    y_raw, dx_raw = pl.pallas_call(
        functools.partial(kernel, (sections, rows, cols, block_rows, block_cols)),
        out_shape=(
            jax.ShapeDtypeStruct((owned, cols * out_width), BF16),
            jax.ShapeDtypeStruct((owned, rows * in_width), BF16),
        ),
        in_specs=[pl.BlockSpec(memory_space=pltpu.SMEM)]
        + [pl.BlockSpec(memory_space=pltpu.MemorySpace.HBM)] * 7,
        out_specs=(pl.BlockSpec(memory_space=pl.ANY), pl.BlockSpec(memory_space=pl.ANY)),
        scratch_shapes=[
            pltpu.SMEM(tok_count.shape, jnp.int32),
            pltpu.VMEM(owner_order.shape, jnp.int32),
            pltpu.VMEM((1, slot_total), jnp.int32),
            pltpu.VMEM((1, slot_total), jnp.int32),
            pltpu.SMEM((1, table), jnp.int32),
            pltpu.VMEM((1, table), jnp.int32),
            pltpu.VMEM((slot_total + 1, blk, blk), BF16),
            pltpu.VMEM((tokens, in_width), BF16),
            pltpu.VMEM((tokens, in_width), BF16),
            pltpu.VMEM((rows, shard, out_width), BF16),
            pltpu.VMEM((FWD_UNITS, 2, tokens // 2, fwd_width), BF16),
            pltpu.VMEM((FWD_UNITS, tokens // 2, fwd_width), BF16),
            pltpu.VMEM((FWD_UNITS, ring, shard, fwd_width), BF16),
            pltpu.VMEM((FWD_UNITS, shard, fwd_width), BF16),
            pltpu.VMEM((FWD_UNITS, shard, fwd_width), BF16),
            pltpu.VMEM((FWD_UNITS, shard, fwd_width), BF16),
            pltpu.VMEM((FWD_UNITS, cols, owned, fwd_width), BF16),
            pltpu.VMEM((BWD_UNITS, cols, rows, owned, bwd_width), BF16),
            pltpu.VMEM((BWD_UNITS, rows, owned, bwd_width), BF16),
            pltpu.VMEM((BWD_UNITS, rows, owned, bwd_width), BF16),
            pltpu.VMEM((BWD_UNITS, rows, owned, bwd_width), BF16),
            pltpu.VMEM((BWD_UNITS // BWD_GROUP, rows, owned, BWD_GROUP * bwd_width), BF16),
            dma((8,)),
            dma((13,)),
            dma((13,)),
            dma((FWD_UNITS,)),
            dma((FWD_UNITS,)),
            dma((FWD_UNITS, 3)),
            dma((FWD_UNITS, 3)),
            dma((FWD_UNITS, cols)),
            dma,
            dma((BWD_UNITS, 3)),
            dma((BWD_UNITS, 3)),
            dma((BWD_UNITS // BWD_GROUP, rows)),
            dma,
        ],
        compiler_params=pltpu.CompilerParams(
            collective_id=0, has_side_effects=True, vmem_limit_bytes=32 * 1024 * 1024
        ),
    )(
        blk_count,
        *[
            pltpu.with_memory_space_constraint(operand, pltpu.MemorySpace.HBM)
            for operand in (
                tok_count,
                owner_order,
                blk_row.reshape(1, slot_total),
                blk_col.reshape(1, slot_total),
                x_fwd,
                dy_bwd,
                w_blocks.reshape(slot_total, blk, blk),
            )
        ],
    )
    section = lax.axis_index("section")
    y_next = jnp.where(section > 0, y_raw, jnp.zeros_like(y_raw))
    dx_section = jnp.where(section >= 0, dx_raw, jnp.zeros_like(dx_raw))
    return (y_next, dx_section)


def solution(mesh):
    return jax.shard_map(
        local,
        mesh=mesh,
        in_specs=(
            P("section", "row"),
            P(("section", "row"), "col"),
            P("section", "row", "col", None, None, None),
            P("section", "row", "col", None),
            P("section", "row", "col", None),
            P("section", "row", "col"),
            P("section", None),
            P("section", None),
        ),
        out_specs=(P(("section", "row", "col"), None), P(("section", "row", "col"), None)),
        check_vma=False,
    )
```

```python
import functools

import jax
import jax.numpy as jnp
from jax import lax
from jax.experimental import pallas as pl
from jax.experimental.pallas import tpu as pltpu
from jax.sharding import PartitionSpec as P

MESH = pl.DeviceIdType.MESH
F32 = jnp.float32
BF16 = jnp.bfloat16
FWD_UNITS = 6
BWD_UNITS = 6
BWD_GROUP = 1
BWD_DOT = 2


def kernel(
    sizes,
    count_ref,
    tok_hbm,
    owner_hbm,
    blk_row_hbm,
    blk_col_hbm,
    x_hbm,
    dy_hbm,
    w_hbm,
    y_out,
    dx_out,
    tok_ref,
    owner_ref,
    blk_row_ref,
    blk_col_ref,
    slot_ref,
    slot_row,
    w,
    x,
    xp,
    dy_all,
    part,
    pair_in,
    summed,
    fwd_relay,
    fwd_direct,
    fwd_comb,
    fwd_fin,
    bpart,
    bwd_relay,
    bwd_direct,
    bwd_comb,
    bwd_fin,
    load_sem,
    gather_send,
    gather_recv,
    pair_send,
    pair_recv,
    fring_send,
    fring_recv,
    ffin_send,
    y_recv,
    bring_send,
    bring_recv,
    bfin_send,
    dx_recv,
):
    sections, rows, cols, block_rows, block_cols = sizes
    blk = w.shape[1]
    slot_total = w_hbm.shape[0]
    tokens, in_width = x.shape
    out_width = dy_all.shape[2]
    shard = dy_all.shape[1]
    fwd_width = out_width // FWD_UNITS
    bwd_width = in_width // BWD_UNITS

    sec = lax.axis_index("section")
    row = lax.axis_index("row")
    col = lax.axis_index("col")
    height, core = row // 2, row % 2
    ring = rows // 2

    def high(by):
        return lax.rem(height + by + ring, ring)

    def across(by):
        return lax.rem(col + by + cols, cols)

    sibling = (sec, height * 2 + 1 - core, col)

    def tall(by):
        return (sec, high(by) * 2 + core, col)

    def wide(by):
        return (sec, row, across(by))

    load_w = pltpu.make_async_copy(w_hbm, w.at[pl.ds(0, slot_total)], load_sem.at[0])
    load_x = pltpu.make_async_copy(x_hbm, x, load_sem.at[1])
    load_dy = pltpu.make_async_copy(dy_hbm, dy_all.at[row], load_sem.at[2])
    load_dy.start()
    small = [
        pltpu.make_async_copy(there, here, load_sem.at[4 + k])
        for k, (there, here) in enumerate(
            (
                (blk_row_hbm, blk_row_ref),
                (blk_col_hbm, blk_col_ref),
                (tok_hbm, tok_ref),
                (owner_hbm, owner_ref),
            )
        )
    ]
    for copy in small:
        copy.start()
    load_x.start()
    load_w.start()

    barrier = pltpu.get_barrier_semaphore()

    def greet(device):
        pl.semaphore_signal(barrier, inc=1, device_id=device, device_id_type=MESH)

    for by in range(1, rows):
        greet((sec, lax.rem(row + by, rows), col))
    greet(wide(1))
    greet(wide(-1))

    @pl.when(sec > 0)
    def _():
        for c in range(cols):
            greet((sec - 1, row, c))


    @pl.when(sec < sections - 1)
    def _():
        pl.semaphore_wait(barrier, rows + 1 + cols)

    @pl.when(sec == sections - 1)
    def _():
        pl.semaphore_wait(barrier, rows + 1)

    def gather(k, src_row, lo, width, device):
        place = dy_all.at[src_row, :, pl.ds(lo, width)]
        return pltpu.make_async_remote_copy(
            src_ref=place,
            dst_ref=place,
            send_sem=gather_send.at[k],
            recv_sem=gather_recv.at[k],
            device_id=device,
            device_id_type=MESH,
        )

    half = out_width // 2
    below, above, far = high(-1) * 2 + core, high(1) * 2 + core, high(2) * 2 + core
    twin = 1 - 2 * core

    load_dy.wait()
    gathers = [
        gather(0, row, 0, half, tall(1)),
        gather(1, row, half, half, tall(-1)),
        gather(2, row, half, half, tall(1)),
        gather(3, row, 0, half, tall(-1)),
        gather(4, row, 0, out_width, sibling),
    ]
    for copy in gathers:
        copy.start()

    def hand_on(*copies):
        for copy in copies:
            copy.start()
            gathers.append(copy)

    for copy in small:
        copy.wait()
    w[slot_total] = jnp.zeros((blk, blk), BF16)

    slot = lax.broadcasted_iota(jnp.int32, (1, slot_total), 1)
    target = blk_row_ref[...] * block_cols + blk_col_ref[...]
    target = jnp.where(slot < count_ref[0, 0, 0], target, -1)
    target = jnp.concatenate([target, jnp.full((1, blk - slot_total), -1, jnp.int32)], axis=1)
    target = jnp.broadcast_to(target, (8, blk)).T[:, 0:1]
    held = jnp.where(
        target == lax.broadcasted_iota(jnp.int32, (blk, slot_row.shape[1]), 1),
        lax.broadcasted_iota(jnp.int32, (blk, slot_row.shape[1]), 0),
        slot_total,
    )
    slot_row[...] = jnp.min(held, axis=0, keepdims=True)
    load_slots = pltpu.make_async_copy(slot_row, slot_ref, load_sem.at[3])
    load_slots.start()
    limit = tok_ref[0, 0]
    blocks = owner_ref.shape[1]
    length = tokens // blocks
    half_rows = tokens // 2

    def delivered(m):
        k = m // half_rows
        rest = m % half_rows
        return ((rest // shard) * 2 + k) * shard + rest % shard

    place = delivered(lax.broadcasted_iota(jnp.int32, (blocks, tokens), 1)) // length
    spread = (place == lax.broadcasted_iota(jnp.int32, (blocks, tokens), 0)).astype(F32).astype(BF16)
    owners = jnp.broadcast_to(owner_ref[...].astype(F32), (8, blocks)).astype(BF16)
    owner_row = jnp.dot(owners, spread, preferred_element_type=F32)
    inner = (lax.broadcasted_iota(jnp.int32, (8, tokens), 1) % length).astype(F32)
    source = owner_row * length + inner
    source = jnp.where(source < limit.astype(F32), source, -1.0).T[:, 0:1]
    token = lax.broadcasted_iota(jnp.int32, (tokens, tokens), 1).astype(F32)
    pick = jnp.where(token == source, 1.0, 0.0).astype(F32).astype(BF16)
    load_x.wait()
    xp[...] = jnp.dot(pick, x[...], preferred_element_type=F32).astype(BF16)
    load_slots.wait()
    load_w.wait()

    def fwd_dot(u):
        def tile(n, carry):
            first = (u * (fwd_width // (2 * blk)) + n) * 2
            rhs = jnp.concatenate(
                [
                    jnp.concatenate(
                        [w[slot_ref[0, r * block_cols + first + j]] for j in range(2)], axis=1
                    )
                    for r in range(block_rows)
                ],
                axis=0,
            )
            out = jnp.dot(xp[...], rhs, preferred_element_type=F32)
            at = pl.ds(pl.multiple_of(n * 2 * blk, 2 * blk), 2 * blk)
            part[u, :, :, at] = out.astype(BF16).reshape(2, half_rows, 2 * blk)
            return carry

        lax.fori_loop(0, fwd_width // (2 * blk), tile, 0, unroll=True)

    def pair_copy(u):
        return pltpu.make_async_remote_copy(
            src_ref=part.at[u, 1 - core],
            dst_ref=pair_in.at[u],
            send_sem=pair_send.at[u],
            recv_sem=pair_recv.at[u],
            device_id=sibling,
            device_id_type=MESH,
        )

    def fwd_ring(u, k):
        way = 1 if u % 2 == 0 else -1
        by, dst, to = ((2, fwd_relay, way), (-way, fwd_direct, -way), (way, fwd_comb, way))[k]
        return pltpu.make_async_remote_copy(
            src_ref=summed.at[u, high(by)],
            dst_ref=dst.at[u],
            send_sem=fring_send.at[u, k],
            recv_sem=fring_recv.at[u, k],
            device_id=tall(to),
            device_id_type=MESH,
        )

    def fwd_pair(u):
        pair_copy(u).wait_recv()
        both = part[u, core].astype(F32) + pair_in[u].astype(F32)
        summed[u] = both.astype(BF16).reshape(ring, shard, fwd_width)
        fwd_ring(u, 0).start()
        fwd_ring(u, 1).start()

    def fwd_mid(u):
        way = 1 if u % 2 == 0 else -1
        fwd_ring(u, 0).wait_recv()
        there = high(way)
        summed[u, there] = (summed[u, there].astype(F32) + fwd_relay[u].astype(F32)).astype(BF16)
        fwd_ring(u, 2).start()

    def y_copy(u, c):
        return pltpu.make_async_remote_copy(
            src_ref=fwd_fin.at[u, c],
            dst_ref=y_out.at[:, pl.ds(pl.multiple_of(col * out_width + u * fwd_width, 128), fwd_width)],
            send_sem=ffin_send.at[u, c],
            recv_sem=y_recv,
            device_id=(sec + 1, row, c),
            device_id_type=MESH,
        )

    def fwd_end(u):
        fwd_ring(u, 1).wait_recv()
        fwd_ring(u, 2).wait_recv()
        total = summed[u, height].astype(F32) + fwd_direct[u].astype(F32) + fwd_comb[u].astype(F32)
        fwd_fin[u] = total.reshape(cols, shard // cols, fwd_width).astype(BF16)

        @pl.when(sec < sections - 1)
        def _():
            for c in range(cols):
                y_copy(u, c).start()

    def bwd_dot(p):
        for v in range(p * BWD_DOT, (p + 1) * BWD_DOT):
            for n in range(bwd_width // (2 * blk)):
                first = (v * (bwd_width // (2 * blk)) + n) * 2
                rhs = jnp.concatenate(
                    [
                        jnp.concatenate(
                            [w[slot_ref[0, (first + j) * block_cols + c]] for j in range(2)], axis=0
                        )
                        for c in range(block_cols)
                    ],
                    axis=1,
                )
                out = lax.dot_general(
                    dy_all[...].reshape(tokens, out_width),
                    rhs,
                    (((1,), (1,)), ((), ())),
                    preferred_element_type=F32,
                )
                out = out.reshape(rows, cols, shard // cols, 2 * blk).astype(BF16)
                for c in range(cols):
                    bpart[v, c, :, :, pl.ds(n * 2 * blk, 2 * blk)] = out[:, c]

    def bwd_ring(v, k):
        way = 1 if v % 2 == 0 else -1
        by, dst, to = ((2, bwd_relay, way), (-way, bwd_direct, -way), (way, bwd_comb, way))[k]
        return pltpu.make_async_remote_copy(
            src_ref=bpart.at[v, across(by)],
            dst_ref=dst.at[v],
            send_sem=bring_send.at[v, k],
            recv_sem=bring_recv.at[v, k],
            device_id=wide(to),
            device_id_type=MESH,
        )

    def bwd_mid(v):
        way = 1 if v % 2 == 0 else -1
        bwd_ring(v, 0).wait_recv()
        there = across(way)
        bpart[v, there] = (bpart[v, there].astype(F32) + bwd_relay[v].astype(F32)).astype(BF16)
        bwd_ring(v, 2).start()

    group_width = BWD_GROUP * bwd_width

    def dx_at(g):
        return dx_out.at[:, pl.ds(pl.multiple_of(row * in_width + g * group_width, 128), group_width)]

    def dx_copy(g, by):
        to = lax.rem(row + by, rows)
        return pltpu.make_async_remote_copy(
            src_ref=bwd_fin.at[g, to],
            dst_ref=dx_at(g),
            send_sem=bfin_send.at[g, by],
            recv_sem=dx_recv,
            device_id=(sec, to, col),
            device_id_type=MESH,
        )

    def dx_own(g):
        return pltpu.make_async_copy(bwd_fin.at[g, row], dx_at(g), bfin_send.at[g, 0])

    def bwd_end(v):
        bwd_ring(v, 1).wait_recv()
        bwd_ring(v, 2).wait_recv()
        total = bpart[v, col].astype(F32) + bwd_direct[v].astype(F32) + bwd_comb[v].astype(F32)
        token = lax.broadcasted_iota(jnp.int32, total.shape, 0) * shard + col * (shard // cols)
        token = token + lax.broadcasted_iota(jnp.int32, total.shape, 1)
        total = jnp.where(token < tok_ref[0, 1], total, 0.0).astype(BF16)
        g = v // BWD_GROUP
        bwd_fin[g, :, :, pl.ds((v % BWD_GROUP) * bwd_width, bwd_width)] = total
        if v % BWD_GROUP == BWD_GROUP - 1:
            for by in range(1, rows):
                dx_copy(g, by).start()
            dx_own(g).start()

    def fwd_first(u):
        fwd_dot(u)
        pair_copy(u).start()

    def bwd_first(p):
        bwd_dot(p)
        for v in range(p * BWD_DOT, (p + 1) * BWD_DOT):
            bwd_ring(v, 0).start()
            bwd_ring(v, 1).start()

    fwd_first(0)
    fwd_first(1)
    fwd_first(2)
    fwd_first(3)
    gather(0, below, 0, half, tall(1)).wait_recv()
    hand_on(gather(5, below, 0, half, tall(1)), gather(6, below, 0, half, sibling))
    gather(1, above, half, half, tall(-1)).wait_recv()
    hand_on(gather(7, above, half, half, tall(-1)), gather(8, above, half, half, sibling))
    fwd_pair(0)
    fwd_pair(1)
    fwd_first(4)
    fwd_pair(2)
    fwd_first(5)
    gather(2, below, half, half, tall(1)).wait_recv()
    hand_on(gather(9, below, half, half, sibling))
    gather(3, above, 0, half, tall(-1)).wait_recv()
    hand_on(gather(10, above, 0, half, sibling))
    gather(5, far, 0, half, tall(1)).wait_recv()
    hand_on(gather(11, far, 0, half, sibling))
    gather(7, far, half, half, tall(-1)).wait_recv()
    hand_on(gather(12, far, half, half, sibling))
    fwd_mid(0)
    fwd_pair(3)
    fwd_mid(1)
    fwd_pair(4)
    gather(4, row + twin, 0, out_width, sibling).wait_recv()
    gather(6, below + twin, 0, half, sibling).wait_recv()
    gather(8, above + twin, half, half, sibling).wait_recv()
    gather(9, below + twin, half, half, sibling).wait_recv()
    gather(10, above + twin, 0, half, sibling).wait_recv()
    gather(11, far + twin, 0, half, sibling).wait_recv()
    gather(12, far + twin, half, half, sibling).wait_recv()
    bwd_first(0)
    bwd_first(1)
    bwd_first(2)
    fwd_mid(2)
    fwd_pair(5)
    bwd_mid(0)
    fwd_mid(3)
    fwd_mid(4)
    fwd_end(0)
    fwd_end(1)
    bwd_mid(1)
    bwd_mid(2)
    bwd_mid(3)
    fwd_end(2)
    bwd_mid(4)
    fwd_mid(5)
    bwd_mid(5)
    fwd_end(3)
    fwd_end(4)
    bwd_end(0)
    bwd_end(1)
    bwd_end(2)
    bwd_end(3)
    fwd_end(5)
    bwd_end(4)
    bwd_end(5)

    for copy in gathers:
        copy.wait_send()
    for u in range(FWD_UNITS):
        pair_copy(u).wait_send()
        for k in range(3):
            fwd_ring(u, k).wait_send()
    for v in range(BWD_UNITS):
        for k in range(3):
            bwd_ring(v, k).wait_send()
    for g in range(BWD_UNITS // BWD_GROUP):
        for by in range(1, rows):
            dx_copy(g, by).wait_send()
        dx_own(g).wait()

    @pl.when(sec < sections - 1)
    def _():
        for u in range(FWD_UNITS):
            for c in range(cols):
                y_copy(u, c).wait_send()

    @pl.when(sec > 0)
    def _():
        pltpu.make_async_remote_copy(
            src_ref=y_out,
            dst_ref=y_out,
            send_sem=y_recv,
            recv_sem=y_recv,
            device_id=sibling,
            device_id_type=MESH,
        ).wait_recv()

    others = dx_out.at[:, pl.ds(0, (rows - 1) * in_width)]
    pltpu.make_async_remote_copy(
        src_ref=others,
        dst_ref=others,
        send_sem=dx_recv,
        recv_sem=dx_recv,
        device_id=sibling,
        device_id_type=MESH,
    ).wait_recv()


def local(x_fwd, dy_bwd, w_blocks, blk_row, blk_col, blk_count, tok_count, owner_order):
    sections = lax.axis_size("section")
    rows = lax.axis_size("row")
    cols = lax.axis_size("col")
    ring = rows // 2
    tokens, in_width = x_fwd.shape
    shard, out_width = dy_bwd.shape
    slot_total = w_blocks.shape[3]
    blk = w_blocks.shape[5]
    block_rows, block_cols = in_width // blk, out_width // blk
    table = pl.cdiv(block_rows * block_cols, 128) * 128
    owned = tokens // (rows * cols)
    fwd_width = out_width // FWD_UNITS
    bwd_width = in_width // BWD_UNITS

    dma = pltpu.SemaphoreType.DMA
    y_raw, dx_raw = pl.pallas_call(
        functools.partial(kernel, (sections, rows, cols, block_rows, block_cols)),
        out_shape=(
            jax.ShapeDtypeStruct((owned, cols * out_width), BF16),
            jax.ShapeDtypeStruct((owned, rows * in_width), BF16),
        ),
        in_specs=[pl.BlockSpec(memory_space=pltpu.SMEM)]
        + [pl.BlockSpec(memory_space=pltpu.MemorySpace.HBM)] * 7,
        out_specs=(pl.BlockSpec(memory_space=pl.ANY), pl.BlockSpec(memory_space=pl.ANY)),
        scratch_shapes=[
            pltpu.SMEM(tok_count.shape, jnp.int32),
            pltpu.VMEM(owner_order.shape, jnp.int32),
            pltpu.VMEM((1, slot_total), jnp.int32),
            pltpu.VMEM((1, slot_total), jnp.int32),
            pltpu.SMEM((1, table), jnp.int32),
            pltpu.VMEM((1, table), jnp.int32),
            pltpu.VMEM((slot_total + 1, blk, blk), BF16),
            pltpu.VMEM((tokens, in_width), BF16),
            pltpu.VMEM((tokens, in_width), BF16),
            pltpu.VMEM((rows, shard, out_width), BF16),
            pltpu.VMEM((FWD_UNITS, 2, tokens // 2, fwd_width), BF16),
            pltpu.VMEM((FWD_UNITS, tokens // 2, fwd_width), BF16),
            pltpu.VMEM((FWD_UNITS, ring, shard, fwd_width), BF16),
            pltpu.VMEM((FWD_UNITS, shard, fwd_width), BF16),
            pltpu.VMEM((FWD_UNITS, shard, fwd_width), BF16),
            pltpu.VMEM((FWD_UNITS, shard, fwd_width), BF16),
            pltpu.VMEM((FWD_UNITS, cols, owned, fwd_width), BF16),
            pltpu.VMEM((BWD_UNITS, cols, rows, owned, bwd_width), BF16),
            pltpu.VMEM((BWD_UNITS, rows, owned, bwd_width), BF16),
            pltpu.VMEM((BWD_UNITS, rows, owned, bwd_width), BF16),
            pltpu.VMEM((BWD_UNITS, rows, owned, bwd_width), BF16),
            pltpu.VMEM((BWD_UNITS // BWD_GROUP, rows, owned, BWD_GROUP * bwd_width), BF16),
            dma((8,)),
            dma((13,)),
            dma((13,)),
            dma((FWD_UNITS,)),
            dma((FWD_UNITS,)),
            dma((FWD_UNITS, 3)),
            dma((FWD_UNITS, 3)),
            dma((FWD_UNITS, cols)),
            dma,
            dma((BWD_UNITS, 3)),
            dma((BWD_UNITS, 3)),
            dma((BWD_UNITS // BWD_GROUP, rows)),
            dma,
        ],
        compiler_params=pltpu.CompilerParams(
            collective_id=0, has_side_effects=True, vmem_limit_bytes=32 * 1024 * 1024
        ),
    )(
        blk_count,
        *[
            pltpu.with_memory_space_constraint(operand, pltpu.MemorySpace.HBM)
            for operand in (
                tok_count,
                owner_order,
                blk_row.reshape(1, slot_total),
                blk_col.reshape(1, slot_total),
                x_fwd,
                dy_bwd,
                w_blocks.reshape(slot_total, blk, blk),
            )
        ],
    )
    section = lax.axis_index("section")
    y_next = jnp.where(section > 0, y_raw, jnp.zeros_like(y_raw))
    dx_section = jnp.where(section >= 0, dx_raw, jnp.zeros_like(dx_raw))
    return (y_next, dx_section)


def solution(mesh):
    return jax.shard_map(
        local,
        mesh=mesh,
        in_specs=(
            P("section", "row"),
            P(("section", "row"), "col"),
            P("section", "row", "col", None, None, None),
            P("section", "row", "col", None),
            P("section", "row", "col", None),
            P("section", "row", "col"),
            P("section", None),
            P("section", None),
        ),
        out_specs=(P(("section", "row", "col"), None), P(("section", "row", "col"), None)),
        check_vma=False,
    )
```

```python
import functools

import jax
import jax.numpy as jnp
from jax import lax
from jax.experimental import pallas as pl
from jax.experimental.pallas import tpu as pltpu
from jax.sharding import PartitionSpec as P

MESH = pl.DeviceIdType.MESH
F32 = jnp.float32
BF16 = jnp.bfloat16
FWD_UNITS = 6
BWD_UNITS = 6
BWD_GROUP = 1
BWD_DOT = 2


def kernel(
    sizes,
    count_ref,
    tok_hbm,
    owner_hbm,
    blk_row_hbm,
    blk_col_hbm,
    x_hbm,
    dy_hbm,
    w_hbm,
    y_out,
    dx_out,
    tok_ref,
    owner_ref,
    blk_row_ref,
    blk_col_ref,
    slot_ref,
    slot_row,
    w,
    x,
    xp,
    dy_all,
    part,
    pair_in,
    summed,
    fwd_relay,
    fwd_direct,
    fwd_comb,
    fwd_fin,
    bpart,
    bwd_relay,
    bwd_direct,
    bwd_comb,
    bwd_fin,
    load_sem,
    gather_send,
    gather_recv,
    pair_send,
    pair_recv,
    fring_send,
    fring_recv,
    ffin_send,
    y_recv,
    bring_send,
    bring_recv,
    bfin_send,
    dx_recv,
    ready,
):
    sections, rows, cols, block_rows, block_cols = sizes
    blk = w.shape[1]
    slot_total = w_hbm.shape[0]
    tokens, in_width = x.shape
    out_width = dy_all.shape[2]
    shard = dy_all.shape[1]
    fwd_width = out_width // FWD_UNITS
    bwd_width = in_width // BWD_UNITS

    sec = lax.axis_index("section")
    row = lax.axis_index("row")
    col = lax.axis_index("col")
    height, core = row // 2, row % 2
    ring = rows // 2

    def high(by):
        return lax.rem(height + by + ring, ring)

    def across(by):
        return lax.rem(col + by + cols, cols)

    sibling = (sec, height * 2 + 1 - core, col)

    def tall(by):
        return (sec, high(by) * 2 + core, col)

    def wide(by):
        return (sec, row, across(by))

    load_w = pltpu.make_async_copy(w_hbm, w.at[pl.ds(0, slot_total)], load_sem.at[0])
    load_x = pltpu.make_async_copy(x_hbm, x, load_sem.at[1])
    load_dy = pltpu.make_async_copy(dy_hbm, dy_all.at[row], load_sem.at[2])
    load_dy.start()
    small = [
        pltpu.make_async_copy(there, here, load_sem.at[4 + k])
        for k, (there, here) in enumerate(
            (
                (blk_row_hbm, blk_row_ref),
                (blk_col_hbm, blk_col_ref),
                (tok_hbm, tok_ref),
                (owner_hbm, owner_ref),
            )
        )
    ]
    for copy in small:
        copy.start()
    load_x.start()
    load_w.start()

    barrier = pltpu.get_barrier_semaphore()

    def greet(device):
        pl.semaphore_signal(barrier, inc=1, device_id=device, device_id_type=MESH)

    for by in range(1, rows):
        greet((sec, lax.rem(row + by, rows), col))
    greet(wide(1))
    greet(wide(-1))

    @pl.when(sec == 1)
    def _():
        for c in range(cols):
            greet((0, row, c))

    @pl.when(jnp.logical_and(sec > 0, sec < sections - 1))
    def _():
        for c in range(cols):
            greet((sec + 1, row, c))


    @pl.when(sec != 1)
    def _():
        pl.semaphore_wait(barrier, rows + 1 + cols)

    @pl.when(sec == 1)
    def _():
        pl.semaphore_wait(barrier, rows + 1)

    def gather(k, src_row, lo, width, device):
        place = dy_all.at[src_row, :, pl.ds(lo, width)]
        return pltpu.make_async_remote_copy(
            src_ref=place,
            dst_ref=place,
            send_sem=gather_send.at[k],
            recv_sem=gather_recv.at[k],
            device_id=device,
            device_id_type=MESH,
        )

    half = out_width // 2
    below, above, far = high(-1) * 2 + core, high(1) * 2 + core, high(2) * 2 + core
    twin = 1 - 2 * core

    load_dy.wait()
    gathers = [
        gather(0, row, 0, half, tall(1)),
        gather(1, row, half, half, tall(-1)),
        gather(2, row, half, half, tall(1)),
        gather(3, row, 0, half, tall(-1)),
        gather(4, row, 0, out_width, sibling),
    ]
    for copy in gathers:
        copy.start()

    def hand_on(*copies):
        for copy in copies:
            copy.start()
            gathers.append(copy)

    @pl.when(sec > 1)
    def _():
        for c in range(cols):
            pl.semaphore_signal(ready, inc=1, device_id=(sec - 1, row, c), device_id_type=MESH)

    for copy in small:
        copy.wait()
    w[slot_total] = jnp.zeros((blk, blk), BF16)

    slot = lax.broadcasted_iota(jnp.int32, (1, slot_total), 1)
    target = blk_row_ref[...] * block_cols + blk_col_ref[...]
    target = jnp.where(slot < count_ref[0, 0, 0], target, -1)
    target = jnp.concatenate([target, jnp.full((1, blk - slot_total), -1, jnp.int32)], axis=1)
    target = jnp.broadcast_to(target, (8, blk)).T[:, 0:1]
    held = jnp.where(
        target == lax.broadcasted_iota(jnp.int32, (blk, slot_row.shape[1]), 1),
        lax.broadcasted_iota(jnp.int32, (blk, slot_row.shape[1]), 0),
        slot_total,
    )
    slot_row[...] = jnp.min(held, axis=0, keepdims=True)
    load_slots = pltpu.make_async_copy(slot_row, slot_ref, load_sem.at[3])
    load_slots.start()
    limit = tok_ref[0, 0]
    blocks = owner_ref.shape[1]
    length = tokens // blocks
    half_rows = tokens // 2

    def delivered(m):
        k = m // half_rows
        rest = m % half_rows
        return ((rest // shard) * 2 + k) * shard + rest % shard

    place = delivered(lax.broadcasted_iota(jnp.int32, (blocks, tokens), 1)) // length
    spread = (place == lax.broadcasted_iota(jnp.int32, (blocks, tokens), 0)).astype(F32).astype(BF16)
    owners = jnp.broadcast_to(owner_ref[...].astype(F32), (8, blocks)).astype(BF16)
    owner_row = jnp.dot(owners, spread, preferred_element_type=F32)
    inner = (lax.broadcasted_iota(jnp.int32, (8, tokens), 1) % length).astype(F32)
    source = owner_row * length + inner
    source = jnp.where(source < limit.astype(F32), source, -1.0).T[:, 0:1]
    token = lax.broadcasted_iota(jnp.int32, (tokens, tokens), 1).astype(F32)
    pick = jnp.where(token == source, 1.0, 0.0).astype(F32).astype(BF16)
    load_x.wait()
    xp[...] = jnp.dot(pick, x[...], preferred_element_type=F32).astype(BF16)
    load_slots.wait()
    load_w.wait()

    def fwd_dot(u):
        def tile(n, carry):
            first = (u * (fwd_width // (2 * blk)) + n) * 2
            rhs = jnp.concatenate(
                [
                    jnp.concatenate(
                        [w[slot_ref[0, r * block_cols + first + j]] for j in range(2)], axis=1
                    )
                    for r in range(block_rows)
                ],
                axis=0,
            )
            out = jnp.dot(xp[...], rhs, preferred_element_type=F32)
            at = pl.ds(pl.multiple_of(n * 2 * blk, 2 * blk), 2 * blk)
            part[u, :, :, at] = out.astype(BF16).reshape(2, half_rows, 2 * blk)
            return carry

        lax.fori_loop(0, fwd_width // (2 * blk), tile, 0, unroll=True)

    def pair_copy(u):
        return pltpu.make_async_remote_copy(
            src_ref=part.at[u, 1 - core],
            dst_ref=pair_in.at[u],
            send_sem=pair_send.at[u],
            recv_sem=pair_recv.at[u],
            device_id=sibling,
            device_id_type=MESH,
        )

    def fwd_ring(u, k):
        way = 1 if u % 2 == 0 else -1
        by, dst, to = ((2, fwd_relay, way), (-way, fwd_direct, -way), (way, fwd_comb, way))[k]
        return pltpu.make_async_remote_copy(
            src_ref=summed.at[u, high(by)],
            dst_ref=dst.at[u],
            send_sem=fring_send.at[u, k],
            recv_sem=fring_recv.at[u, k],
            device_id=tall(to),
            device_id_type=MESH,
        )

    def fwd_pair(u):
        pair_copy(u).wait_recv()
        both = part[u, core].astype(F32) + pair_in[u].astype(F32)
        summed[u] = both.astype(BF16).reshape(ring, shard, fwd_width)
        fwd_ring(u, 0).start()
        fwd_ring(u, 1).start()

    def fwd_mid(u):
        way = 1 if u % 2 == 0 else -1
        fwd_ring(u, 0).wait_recv()
        there = high(way)
        summed[u, there] = (summed[u, there].astype(F32) + fwd_relay[u].astype(F32)).astype(BF16)
        fwd_ring(u, 2).start()

    def y_copy(u, c):
        return pltpu.make_async_remote_copy(
            src_ref=fwd_fin.at[u, c],
            dst_ref=y_out.at[:, pl.ds(pl.multiple_of(col * out_width + u * fwd_width, 128), fwd_width)],
            send_sem=ffin_send.at[u, c],
            recv_sem=y_recv,
            device_id=(sec + 1, row, c),
            device_id_type=MESH,
        )

    def fwd_end(u):
        fwd_ring(u, 1).wait_recv()
        fwd_ring(u, 2).wait_recv()
        total = summed[u, height].astype(F32) + fwd_direct[u].astype(F32) + fwd_comb[u].astype(F32)
        fwd_fin[u] = total.reshape(cols, shard // cols, fwd_width).astype(BF16)

        @pl.when(sec < sections - 1)
        def _():
            for c in range(cols):
                y_copy(u, c).start()

    def bwd_dot(p):
        for v in range(p * BWD_DOT, (p + 1) * BWD_DOT):
            for n in range(bwd_width // (2 * blk)):
                first = (v * (bwd_width // (2 * blk)) + n) * 2
                rhs = jnp.concatenate(
                    [
                        jnp.concatenate(
                            [w[slot_ref[0, (first + j) * block_cols + c]] for j in range(2)], axis=0
                        )
                        for c in range(block_cols)
                    ],
                    axis=1,
                )
                out = lax.dot_general(
                    dy_all[...].reshape(tokens, out_width),
                    rhs,
                    (((1,), (1,)), ((), ())),
                    preferred_element_type=F32,
                )
                out = out.reshape(rows, cols, shard // cols, 2 * blk).astype(BF16)
                for c in range(cols):
                    bpart[v, c, :, :, pl.ds(n * 2 * blk, 2 * blk)] = out[:, c]

    def bwd_ring(v, k):
        way = 1 if v % 2 == 0 else -1
        by, dst, to = ((2, bwd_relay, way), (-way, bwd_direct, -way), (way, bwd_comb, way))[k]
        return pltpu.make_async_remote_copy(
            src_ref=bpart.at[v, across(by)],
            dst_ref=dst.at[v],
            send_sem=bring_send.at[v, k],
            recv_sem=bring_recv.at[v, k],
            device_id=wide(to),
            device_id_type=MESH,
        )

    def bwd_mid(v):
        way = 1 if v % 2 == 0 else -1
        bwd_ring(v, 0).wait_recv()
        there = across(way)
        bpart[v, there] = (bpart[v, there].astype(F32) + bwd_relay[v].astype(F32)).astype(BF16)
        bwd_ring(v, 2).start()

    group_width = BWD_GROUP * bwd_width

    def dx_at(g):
        return dx_out.at[:, pl.ds(pl.multiple_of(row * in_width + g * group_width, 128), group_width)]

    def dx_copy(g, by):
        to = lax.rem(row + by, rows)
        return pltpu.make_async_remote_copy(
            src_ref=bwd_fin.at[g, to],
            dst_ref=dx_at(g),
            send_sem=bfin_send.at[g, by],
            recv_sem=dx_recv,
            device_id=(sec, to, col),
            device_id_type=MESH,
        )

    def dx_own(g):
        return pltpu.make_async_copy(bwd_fin.at[g, row], dx_at(g), bfin_send.at[g, 0])

    def bwd_end(v):
        bwd_ring(v, 1).wait_recv()
        bwd_ring(v, 2).wait_recv()
        total = bpart[v, col].astype(F32) + bwd_direct[v].astype(F32) + bwd_comb[v].astype(F32)
        token = lax.broadcasted_iota(jnp.int32, total.shape, 0) * shard + col * (shard // cols)
        token = token + lax.broadcasted_iota(jnp.int32, total.shape, 1)
        total = jnp.where(token < tok_ref[0, 1], total, 0.0).astype(BF16)
        g = v // BWD_GROUP
        bwd_fin[g, :, :, pl.ds((v % BWD_GROUP) * bwd_width, bwd_width)] = total
        if v % BWD_GROUP == BWD_GROUP - 1:
            for by in range(1, rows):
                dx_copy(g, by).start()
            dx_own(g).start()

    def fwd_first(u):
        fwd_dot(u)
        pair_copy(u).start()

    def bwd_first(p):
        bwd_dot(p)
        for v in range(p * BWD_DOT, (p + 1) * BWD_DOT):
            bwd_ring(v, 0).start()
            bwd_ring(v, 1).start()

    fwd_first(0)
    fwd_first(1)
    fwd_first(2)
    fwd_first(3)
    gather(0, below, 0, half, tall(1)).wait_recv()
    hand_on(gather(5, below, 0, half, tall(1)), gather(6, below, 0, half, sibling))
    gather(1, above, half, half, tall(-1)).wait_recv()
    hand_on(gather(7, above, half, half, tall(-1)), gather(8, above, half, half, sibling))
    fwd_pair(0)
    fwd_pair(1)
    fwd_first(4)
    fwd_pair(2)
    fwd_first(5)
    gather(2, below, half, half, tall(1)).wait_recv()
    hand_on(gather(9, below, half, half, sibling))
    gather(3, above, 0, half, tall(-1)).wait_recv()
    hand_on(gather(10, above, 0, half, sibling))
    gather(5, far, 0, half, tall(1)).wait_recv()
    hand_on(gather(11, far, 0, half, sibling))
    gather(7, far, half, half, tall(-1)).wait_recv()
    hand_on(gather(12, far, half, half, sibling))
    fwd_mid(0)
    fwd_pair(3)
    fwd_mid(1)
    fwd_pair(4)
    gather(4, row + twin, 0, out_width, sibling).wait_recv()
    gather(6, below + twin, 0, half, sibling).wait_recv()
    gather(8, above + twin, half, half, sibling).wait_recv()
    gather(9, below + twin, half, half, sibling).wait_recv()
    gather(10, above + twin, 0, half, sibling).wait_recv()
    gather(11, far + twin, 0, half, sibling).wait_recv()
    gather(12, far + twin, half, half, sibling).wait_recv()
    bwd_first(0)
    bwd_first(1)
    bwd_first(2)
    fwd_mid(2)
    fwd_pair(5)
    bwd_mid(0)
    fwd_mid(3)
    fwd_mid(4)

    @pl.when(jnp.logical_and(sec > 0, sec < sections - 1))
    def _():
        pl.semaphore_wait(ready, cols)

    fwd_end(0)
    fwd_end(1)
    bwd_mid(1)
    bwd_mid(2)
    bwd_mid(3)
    fwd_end(2)
    bwd_mid(4)
    fwd_mid(5)
    bwd_mid(5)
    fwd_end(3)
    fwd_end(4)
    bwd_end(0)
    bwd_end(1)
    bwd_end(2)
    bwd_end(3)
    fwd_end(5)
    bwd_end(4)
    bwd_end(5)

    for copy in gathers:
        copy.wait_send()
    for u in range(FWD_UNITS):
        pair_copy(u).wait_send()
        for k in range(3):
            fwd_ring(u, k).wait_send()
    for v in range(BWD_UNITS):
        for k in range(3):
            bwd_ring(v, k).wait_send()
    for g in range(BWD_UNITS // BWD_GROUP):
        for by in range(1, rows):
            dx_copy(g, by).wait_send()
        dx_own(g).wait()

    @pl.when(sec < sections - 1)
    def _():
        for u in range(FWD_UNITS):
            for c in range(cols):
                y_copy(u, c).wait_send()

    @pl.when(sec > 0)
    def _():
        pltpu.make_async_remote_copy(
            src_ref=y_out,
            dst_ref=y_out,
            send_sem=y_recv,
            recv_sem=y_recv,
            device_id=sibling,
            device_id_type=MESH,
        ).wait_recv()

    others = dx_out.at[:, pl.ds(0, (rows - 1) * in_width)]
    pltpu.make_async_remote_copy(
        src_ref=others,
        dst_ref=others,
        send_sem=dx_recv,
        recv_sem=dx_recv,
        device_id=sibling,
        device_id_type=MESH,
    ).wait_recv()


def local(x_fwd, dy_bwd, w_blocks, blk_row, blk_col, blk_count, tok_count, owner_order):
    sections = lax.axis_size("section")
    rows = lax.axis_size("row")
    cols = lax.axis_size("col")
    ring = rows // 2
    tokens, in_width = x_fwd.shape
    shard, out_width = dy_bwd.shape
    slot_total = w_blocks.shape[3]
    blk = w_blocks.shape[5]
    block_rows, block_cols = in_width // blk, out_width // blk
    table = pl.cdiv(block_rows * block_cols, 128) * 128
    owned = tokens // (rows * cols)
    fwd_width = out_width // FWD_UNITS
    bwd_width = in_width // BWD_UNITS

    dma = pltpu.SemaphoreType.DMA
    y_raw, dx_raw = pl.pallas_call(
        functools.partial(kernel, (sections, rows, cols, block_rows, block_cols)),
        out_shape=(
            jax.ShapeDtypeStruct((owned, cols * out_width), BF16),
            jax.ShapeDtypeStruct((owned, rows * in_width), BF16),
        ),
        in_specs=[pl.BlockSpec(memory_space=pltpu.SMEM)]
        + [pl.BlockSpec(memory_space=pltpu.MemorySpace.HBM)] * 7,
        out_specs=(pl.BlockSpec(memory_space=pl.ANY), pl.BlockSpec(memory_space=pl.ANY)),
        scratch_shapes=[
            pltpu.SMEM(tok_count.shape, jnp.int32),
            pltpu.VMEM(owner_order.shape, jnp.int32),
            pltpu.VMEM((1, slot_total), jnp.int32),
            pltpu.VMEM((1, slot_total), jnp.int32),
            pltpu.SMEM((1, table), jnp.int32),
            pltpu.VMEM((1, table), jnp.int32),
            pltpu.VMEM((slot_total + 1, blk, blk), BF16),
            pltpu.VMEM((tokens, in_width), BF16),
            pltpu.VMEM((tokens, in_width), BF16),
            pltpu.VMEM((rows, shard, out_width), BF16),
            pltpu.VMEM((FWD_UNITS, 2, tokens // 2, fwd_width), BF16),
            pltpu.VMEM((FWD_UNITS, tokens // 2, fwd_width), BF16),
            pltpu.VMEM((FWD_UNITS, ring, shard, fwd_width), BF16),
            pltpu.VMEM((FWD_UNITS, shard, fwd_width), BF16),
            pltpu.VMEM((FWD_UNITS, shard, fwd_width), BF16),
            pltpu.VMEM((FWD_UNITS, shard, fwd_width), BF16),
            pltpu.VMEM((FWD_UNITS, cols, owned, fwd_width), BF16),
            pltpu.VMEM((BWD_UNITS, cols, rows, owned, bwd_width), BF16),
            pltpu.VMEM((BWD_UNITS, rows, owned, bwd_width), BF16),
            pltpu.VMEM((BWD_UNITS, rows, owned, bwd_width), BF16),
            pltpu.VMEM((BWD_UNITS, rows, owned, bwd_width), BF16),
            pltpu.VMEM((BWD_UNITS // BWD_GROUP, rows, owned, BWD_GROUP * bwd_width), BF16),
            dma((8,)),
            dma((13,)),
            dma((13,)),
            dma((FWD_UNITS,)),
            dma((FWD_UNITS,)),
            dma((FWD_UNITS, 3)),
            dma((FWD_UNITS, 3)),
            dma((FWD_UNITS, cols)),
            dma,
            dma((BWD_UNITS, 3)),
            dma((BWD_UNITS, 3)),
            dma((BWD_UNITS // BWD_GROUP, rows)),
            dma,
            pltpu.SemaphoreType.REGULAR,
        ],
        compiler_params=pltpu.CompilerParams(
            collective_id=0, has_side_effects=True, vmem_limit_bytes=32 * 1024 * 1024
        ),
    )(
        blk_count,
        *[
            pltpu.with_memory_space_constraint(operand, pltpu.MemorySpace.HBM)
            for operand in (
                tok_count,
                owner_order,
                blk_row.reshape(1, slot_total),
                blk_col.reshape(1, slot_total),
                x_fwd,
                dy_bwd,
                w_blocks.reshape(slot_total, blk, blk),
            )
        ],
    )
    section = lax.axis_index("section")
    y_next = jnp.where(section > 0, y_raw, jnp.zeros_like(y_raw))
    dx_section = jnp.where(section >= 0, dx_raw, jnp.zeros_like(dx_raw))
    return (y_next, dx_section)


def solution(mesh):
    return jax.shard_map(
        local,
        mesh=mesh,
        in_specs=(
            P("section", "row"),
            P(("section", "row"), "col"),
            P("section", "row", "col", None, None, None),
            P("section", "row", "col", None),
            P("section", "row", "col", None),
            P("section", "row", "col"),
            P("section", None),
            P("section", None),
        ),
        out_specs=(P(("section", "row", "col"), None), P(("section", "row", "col"), None)),
        check_vma=False,
    )
```

```python
import functools

import jax
import jax.numpy as jnp
from jax import lax
from jax.experimental import pallas as pl
from jax.experimental.pallas import tpu as pltpu
from jax.sharding import PartitionSpec as P

MESH = pl.DeviceIdType.MESH
F32 = jnp.float32
BF16 = jnp.bfloat16
FWD_UNITS = 6
BWD_UNITS = 6
BWD_GROUP = 1
BWD_DOT = 2
FAR_UNITS = 2
NEAR = 6


def kernel(
    sizes,
    count_ref,
    tok_hbm,
    owner_hbm,
    blk_row_hbm,
    blk_col_hbm,
    x_hbm,
    dy_hbm,
    w_hbm,
    y_out,
    dx_out,
    tok_ref,
    owner_ref,
    blk_row_ref,
    blk_col_ref,
    slot_ref,
    slot_row,
    w,
    x,
    xp,
    dy_all,
    part,
    pair_in,
    summed,
    fwd_relay,
    fwd_direct,
    fwd_comb,
    fwd_fin,
    bpart,
    bwd_relay,
    bwd_direct,
    bwd_comb,
    bwd_fin,
    fpart,
    far_in,
    far_fin,
    load_sem,
    gather_send,
    gather_recv,
    pair_send,
    pair_recv,
    fring_send,
    fring_recv,
    ffin_send,
    y_recv,
    bring_send,
    bring_recv,
    bfin_send,
    far_send,
    far_recv,
    dx_recv,
    ready,
):
    sections, rows, cols, block_rows, block_cols = sizes
    blk = w.shape[1]
    slot_total = w_hbm.shape[0]
    tokens, in_width = x.shape
    out_width = dy_all.shape[2]
    shard = dy_all.shape[1]
    fwd_width = out_width // FWD_UNITS
    bwd_width = in_width // BWD_UNITS

    sec = lax.axis_index("section")
    row = lax.axis_index("row")
    col = lax.axis_index("col")
    height, core = row // 2, row % 2
    ring = rows // 2

    def high(by):
        return lax.rem(height + by + ring, ring)

    def across(by):
        return lax.rem(col + by + cols, cols)

    sibling = (sec, height * 2 + 1 - core, col)

    def tall(by):
        return (sec, high(by) * 2 + core, col)

    def wide(by):
        return (sec, row, across(by))

    load_w = pltpu.make_async_copy(w_hbm, w.at[pl.ds(0, slot_total)], load_sem.at[0])
    load_x = pltpu.make_async_copy(x_hbm, x, load_sem.at[1])
    load_dy = pltpu.make_async_copy(dy_hbm, dy_all.at[core], load_sem.at[2])
    load_dy.start()
    small = [
        pltpu.make_async_copy(there, here, load_sem.at[4 + k])
        for k, (there, here) in enumerate(
            (
                (blk_row_hbm, blk_row_ref),
                (blk_col_hbm, blk_col_ref),
                (tok_hbm, tok_ref),
                (owner_hbm, owner_ref),
            )
        )
    ]
    for copy in small:
        copy.start()
    load_x.start()
    load_w.start()

    barrier = pltpu.get_barrier_semaphore()

    def greet(device):
        pl.semaphore_signal(barrier, inc=1, device_id=device, device_id_type=MESH)

    for by in range(1, rows):
        greet((sec, lax.rem(row + by, rows), col))
    greet(wide(1))
    greet(wide(-1))

    @pl.when(sec == 1)
    def _():
        for c in range(cols):
            greet((0, row, c))

    @pl.when(jnp.logical_and(sec > 0, sec < sections - 1))
    def _():
        for c in range(cols):
            greet((sec + 1, row, c))


    @pl.when(sec != 1)
    def _():
        pl.semaphore_wait(barrier, rows + 1 + cols)

    @pl.when(sec == 1)
    def _():
        pl.semaphore_wait(barrier, rows + 1)

    OWN, ABOVE, BELOW, FAR = 0, 2, 4, 6

    def gather(k, held, there, lo, width, device):
        return pltpu.make_async_remote_copy(
            src_ref=dy_all.at[held, :, pl.ds(lo, width)],
            dst_ref=dy_all.at[there, :, pl.ds(lo, width)],
            send_sem=gather_send.at[k],
            recv_sem=gather_recv.at[k],
            device_id=device,
            device_id_type=MESH,
        )

    half = out_width // 2

    def arrived(k, held, lo, width):
        gather(k, held + core, held + core, lo, width, sibling).wait_recv()

    def crossed(k, held, lo, width):
        gather(k, held + 1 - core, held + 1 - core, lo, width, sibling).wait_recv()

    def relay(k, held, lo, width):
        return gather(k, held + core, held + core, lo, width, sibling)

    load_dy.wait()
    gathers = [
        gather(0, core, BELOW + core, 0, half, tall(1)),
        gather(1, core, ABOVE + core, half, half, tall(-1)),
        gather(2, core, BELOW + core, half, half, tall(1)),
        gather(3, core, ABOVE + core, 0, half, tall(-1)),
        relay(4, OWN, 0, out_width),
    ]
    for copy in gathers:
        copy.start()

    def hand_on(*copies):
        for copy in copies:
            copy.start()
            gathers.append(copy)

    @pl.when(sec > 1)
    def _():
        for c in range(cols):
            pl.semaphore_signal(ready, inc=1, device_id=(sec - 1, row, c), device_id_type=MESH)

    for copy in small:
        copy.wait()
    w[slot_total] = jnp.zeros((blk, blk), BF16)

    slot = lax.broadcasted_iota(jnp.int32, (1, slot_total), 1)
    target = blk_row_ref[...] * block_cols + blk_col_ref[...]
    target = jnp.where(slot < count_ref[0, 0, 0], target, -1)
    target = jnp.concatenate([target, jnp.full((1, blk - slot_total), -1, jnp.int32)], axis=1)
    target = jnp.broadcast_to(target, (8, blk)).T[:, 0:1]
    held = jnp.where(
        target == lax.broadcasted_iota(jnp.int32, (blk, slot_row.shape[1]), 1),
        lax.broadcasted_iota(jnp.int32, (blk, slot_row.shape[1]), 0),
        slot_total,
    )
    slot_row[...] = jnp.min(held, axis=0, keepdims=True)
    load_slots = pltpu.make_async_copy(slot_row, slot_ref, load_sem.at[3])
    load_slots.start()
    limit = tok_ref[0, 0]
    blocks = owner_ref.shape[1]
    length = tokens // blocks
    half_rows = tokens // 2

    def delivered(m):
        k = m // half_rows
        rest = m % half_rows
        return ((rest // shard) * 2 + k) * shard + rest % shard

    place = delivered(lax.broadcasted_iota(jnp.int32, (blocks, tokens), 1)) // length
    spread = (place == lax.broadcasted_iota(jnp.int32, (blocks, tokens), 0)).astype(F32).astype(BF16)
    owners = jnp.broadcast_to(owner_ref[...].astype(F32), (8, blocks)).astype(BF16)
    owner_row = jnp.dot(owners, spread, preferred_element_type=F32)
    inner = (lax.broadcasted_iota(jnp.int32, (8, tokens), 1) % length).astype(F32)
    source = owner_row * length + inner
    source = jnp.where(source < limit.astype(F32), source, -1.0).T[:, 0:1]
    token = lax.broadcasted_iota(jnp.int32, (tokens, tokens), 1).astype(F32)
    pick = jnp.where(token == source, 1.0, 0.0).astype(F32).astype(BF16)
    load_x.wait()
    xp[...] = jnp.dot(pick, x[...], preferred_element_type=F32).astype(BF16)
    load_slots.wait()
    load_w.wait()

    def fwd_dot(u):
        def tile(n, carry):
            first = (u * (fwd_width // (2 * blk)) + n) * 2
            rhs = jnp.concatenate(
                [
                    jnp.concatenate(
                        [w[slot_ref[0, r * block_cols + first + j]] for j in range(2)], axis=1
                    )
                    for r in range(block_rows)
                ],
                axis=0,
            )
            out = jnp.dot(xp[...], rhs, preferred_element_type=F32)
            at = pl.ds(pl.multiple_of(n * 2 * blk, 2 * blk), 2 * blk)
            part[u, :, :, at] = out.astype(BF16).reshape(2, half_rows, 2 * blk)
            return carry

        lax.fori_loop(0, fwd_width // (2 * blk), tile, 0, unroll=True)

    def pair_copy(u):
        return pltpu.make_async_remote_copy(
            src_ref=part.at[u, 1 - core],
            dst_ref=pair_in.at[u],
            send_sem=pair_send.at[u],
            recv_sem=pair_recv.at[u],
            device_id=sibling,
            device_id_type=MESH,
        )

    def fwd_ring(u, k):
        way = 1 if u % 2 == 0 else -1
        by, dst, to = ((2, fwd_relay, way), (-way, fwd_direct, -way), (way, fwd_comb, way))[k]
        return pltpu.make_async_remote_copy(
            src_ref=summed.at[u, high(by)],
            dst_ref=dst.at[u],
            send_sem=fring_send.at[u, k],
            recv_sem=fring_recv.at[u, k],
            device_id=tall(to),
            device_id_type=MESH,
        )

    def fwd_pair(u):
        pair_copy(u).wait_recv()
        both = part[u, core].astype(F32) + pair_in[u].astype(F32)
        summed[u] = both.astype(BF16).reshape(ring, shard, fwd_width)
        fwd_ring(u, 0).start()
        fwd_ring(u, 1).start()

    def fwd_mid(u):
        way = 1 if u % 2 == 0 else -1
        fwd_ring(u, 0).wait_recv()
        there = high(way)
        summed[u, there] = (summed[u, there].astype(F32) + fwd_relay[u].astype(F32)).astype(BF16)
        fwd_ring(u, 2).start()

    def y_copy(u, c):
        return pltpu.make_async_remote_copy(
            src_ref=fwd_fin.at[u, c],
            dst_ref=y_out.at[:, pl.ds(pl.multiple_of(col * out_width + u * fwd_width, 128), fwd_width)],
            send_sem=ffin_send.at[u, c],
            recv_sem=y_recv,
            device_id=(sec + 1, row, c),
            device_id_type=MESH,
        )

    def fwd_end(u):
        fwd_ring(u, 1).wait_recv()
        fwd_ring(u, 2).wait_recv()
        total = summed[u, height].astype(F32) + fwd_direct[u].astype(F32) + fwd_comb[u].astype(F32)
        fwd_fin[u] = total.reshape(cols, shard // cols, fwd_width).astype(BF16)

        @pl.when(sec < sections - 1)
        def _():
            for c in range(cols):
                y_copy(u, c).start()

    def bwd_tile(first, lo, hi):
        rhs = jnp.concatenate(
            [
                jnp.concatenate(
                    [w[slot_ref[0, (first + j) * block_cols + c]] for j in range(2)], axis=0
                )
                for c in range(block_cols)
            ],
            axis=1,
        )
        out = lax.dot_general(
            dy_all[lo:hi].reshape((hi - lo) * shard, out_width),
            rhs,
            (((1,), (1,)), ((), ())),
            preferred_element_type=F32,
        )
        return out.reshape(hi - lo, cols, shard // cols, 2 * blk).astype(BF16)

    def bwd_dot(p):
        for v in range(p * BWD_DOT, (p + 1) * BWD_DOT):
            for n in range(bwd_width // (2 * blk)):
                out = bwd_tile((v * (bwd_width // (2 * blk)) + n) * 2, 0, NEAR)
                for c in range(cols):
                    bpart[v, c, :, :, pl.ds(n * 2 * blk, 2 * blk)] = out[:, c]

    far_width = in_width // FAR_UNITS

    def far_copy(g, by):
        return pltpu.make_async_remote_copy(
            src_ref=fpart.at[g, across(by)],
            dst_ref=far_in.at[g, by - 1],
            send_sem=far_send.at[g, by - 1],
            recv_sem=far_recv.at[g, by - 1],
            device_id=wide(by),
            device_id_type=MESH,
        )

    def far_first(g):
        def tile(n, carry):
            out = bwd_tile((g * (far_width // (2 * blk)) + n) * 2, NEAR, rows)
            at = pl.ds(pl.multiple_of(n * 2 * blk, 2 * blk), 2 * blk)
            for c in range(cols):
                fpart[g, c, :, :, at] = out[:, c]
            return carry

        lax.fori_loop(0, far_width // (2 * blk), tile, 0, unroll=True)
        for by in (2, 1, 3):
            far_copy(g, by).start()

    def bwd_ring(v, k):
        way = 1 if v % 2 == 0 else -1
        by, dst, to = ((2, bwd_relay, way), (-way, bwd_direct, -way), (way, bwd_comb, way))[k]
        return pltpu.make_async_remote_copy(
            src_ref=bpart.at[v, across(by)],
            dst_ref=dst.at[v],
            send_sem=bring_send.at[v, k],
            recv_sem=bring_recv.at[v, k],
            device_id=wide(to),
            device_id_type=MESH,
        )

    def bwd_mid(v):
        way = 1 if v % 2 == 0 else -1
        bwd_ring(v, 0).wait_recv()
        there = across(way)
        bpart[v, there] = (bpart[v, there].astype(F32) + bwd_relay[v].astype(F32)).astype(BF16)
        bwd_ring(v, 2).start()

    group_width = BWD_GROUP * bwd_width

    def home(q):
        return high((0, 1, -1, 2)[q // 2]) * 2 + q % 2

    def kept(q, total):
        token = home(q) * shard + col * (shard // cols) + lax.broadcasted_iota(jnp.int32, total.shape, 0)
        return jnp.where(token < tok_ref[0, 1], total, 0.0).astype(BF16)

    def dx_at(lo, width):
        return dx_out.at[:, pl.ds(pl.multiple_of(row * in_width + lo, 128), width)]

    def dx_copy(g, q):
        return pltpu.make_async_remote_copy(
            src_ref=bwd_fin.at[g, q],
            dst_ref=dx_at(g * group_width, group_width),
            send_sem=bfin_send.at[g, q],
            recv_sem=dx_recv,
            device_id=(sec, home(q), col),
            device_id_type=MESH,
        )

    def dx_sibling(g):
        return pltpu.make_async_remote_copy(
            src_ref=bwd_fin.at[g, 1 - core],
            dst_ref=dx_at(g * group_width, group_width),
            send_sem=bfin_send.at[g, 1],
            recv_sem=dx_recv,
            device_id=sibling,
            device_id_type=MESH,
        )

    def dx_own(g):
        return pltpu.make_async_copy(
            bwd_fin.at[g, core], dx_at(g * group_width, group_width), bfin_send.at[g, 0]
        )

    def dx_far(g, k):
        return pltpu.make_async_remote_copy(
            src_ref=far_fin.at[g, k],
            dst_ref=dx_at(g * far_width, far_width),
            send_sem=far_send.at[g, 3 + k],
            recv_sem=dx_recv,
            device_id=(sec, home(NEAR + k), col),
            device_id_type=MESH,
        )

    def bwd_end(v):
        bwd_ring(v, 1).wait_recv()
        bwd_ring(v, 2).wait_recv()
        total = bpart[v, col].astype(F32) + bwd_direct[v].astype(F32) + bwd_comb[v].astype(F32)
        g = v // BWD_GROUP
        at = pl.ds((v % BWD_GROUP) * bwd_width, bwd_width)
        for q in range(NEAR):
            bwd_fin[g, q, :, at] = kept(q, total[q])
        if v % BWD_GROUP == BWD_GROUP - 1:
            for q in range(2, NEAR):
                dx_copy(g, q).start()
            dx_sibling(g).start()
            dx_own(g).start()

    def far_end(g):
        total = fpart[g, col].astype(F32)
        for by in (1, 2, 3):
            far_copy(g, by).wait_recv()
            total = total + far_in[g, by - 1].astype(F32)
        for k in range(2):
            far_fin[g, k] = kept(NEAR + k, total[k])
            dx_far(g, k).start()

    def fwd_first(u):
        fwd_dot(u)
        pair_copy(u).start()

    def bwd_first(p):
        bwd_dot(p)
        for v in range(p * BWD_DOT, (p + 1) * BWD_DOT):
            bwd_ring(v, 0).start()
            bwd_ring(v, 1).start()

    fwd_first(0)
    fwd_first(1)
    fwd_first(2)
    fwd_first(3)
    arrived(0, BELOW, 0, half)
    hand_on(gather(5, BELOW + core, FAR + core, 0, half, tall(1)), relay(6, BELOW, 0, half))
    arrived(1, ABOVE, half, half)
    hand_on(gather(7, ABOVE + core, FAR + core, half, half, tall(-1)), relay(8, ABOVE, half, half))
    fwd_pair(0)
    fwd_pair(1)
    fwd_first(4)
    fwd_pair(2)
    fwd_first(5)
    arrived(2, BELOW, half, half)
    hand_on(relay(9, BELOW, half, half))
    arrived(3, ABOVE, 0, half)
    hand_on(relay(10, ABOVE, 0, half))
    fwd_pair(3)
    fwd_pair(4)
    fwd_pair(5)
    crossed(4, OWN, 0, out_width)
    crossed(6, BELOW, 0, half)
    crossed(8, ABOVE, half, half)
    crossed(9, BELOW, half, half)
    crossed(10, ABOVE, 0, half)
    bwd_first(0)
    arrived(5, FAR, 0, half)
    hand_on(relay(11, FAR, 0, half))
    arrived(7, FAR, half, half)
    hand_on(relay(12, FAR, half, half))
    fwd_mid(0)
    bwd_first(1)
    fwd_mid(1)
    fwd_mid(2)
    fwd_mid(3)
    bwd_first(2)
    bwd_mid(0)
    bwd_mid(1)
    fwd_mid(4)
    fwd_mid(5)
    crossed(11, FAR, 0, half)
    crossed(12, FAR, half, half)
    far_first(0)
    bwd_mid(2)

    @pl.when(jnp.logical_and(sec > 0, sec < sections - 1))
    def _():
        pl.semaphore_wait(ready, cols)

    fwd_end(0)
    fwd_end(1)
    bwd_mid(3)
    fwd_end(2)
    far_first(1)
    bwd_mid(4)
    fwd_end(3)
    fwd_end(4)
    bwd_mid(5)
    fwd_end(5)
    bwd_end(0)
    bwd_end(1)
    bwd_end(2)
    far_end(0)
    bwd_end(3)
    far_end(1)
    bwd_end(4)
    bwd_end(5)

    for copy in gathers:
        copy.wait_send()
    for u in range(FWD_UNITS):
        pair_copy(u).wait_send()
        for k in range(3):
            fwd_ring(u, k).wait_send()
    for v in range(BWD_UNITS):
        for k in range(3):
            bwd_ring(v, k).wait_send()
    for g in range(BWD_UNITS // BWD_GROUP):
        for q in range(2, NEAR):
            dx_copy(g, q).wait_send()
        dx_sibling(g).wait_send()
        dx_own(g).wait()
    for g in range(FAR_UNITS):
        for by in (1, 2, 3):
            far_copy(g, by).wait_send()
        for k in range(2):
            dx_far(g, k).wait_send()

    @pl.when(sec < sections - 1)
    def _():
        for u in range(FWD_UNITS):
            for c in range(cols):
                y_copy(u, c).wait_send()

    @pl.when(sec > 0)
    def _():
        pltpu.make_async_remote_copy(
            src_ref=y_out,
            dst_ref=y_out,
            send_sem=y_recv,
            recv_sem=y_recv,
            device_id=sibling,
            device_id_type=MESH,
        ).wait_recv()

    others = dx_out.at[:, pl.ds(0, (rows - 1) * in_width)]
    pltpu.make_async_remote_copy(
        src_ref=others,
        dst_ref=others,
        send_sem=dx_recv,
        recv_sem=dx_recv,
        device_id=sibling,
        device_id_type=MESH,
    ).wait_recv()


def local(x_fwd, dy_bwd, w_blocks, blk_row, blk_col, blk_count, tok_count, owner_order):
    sections = lax.axis_size("section")
    rows = lax.axis_size("row")
    cols = lax.axis_size("col")
    ring = rows // 2
    tokens, in_width = x_fwd.shape
    shard, out_width = dy_bwd.shape
    slot_total = w_blocks.shape[3]
    blk = w_blocks.shape[5]
    block_rows, block_cols = in_width // blk, out_width // blk
    table = pl.cdiv(block_rows * block_cols, 128) * 128
    owned = tokens // (rows * cols)
    fwd_width = out_width // FWD_UNITS
    bwd_width = in_width // BWD_UNITS
    far_width = in_width // FAR_UNITS

    dma = pltpu.SemaphoreType.DMA
    y_raw, dx_raw = pl.pallas_call(
        functools.partial(kernel, (sections, rows, cols, block_rows, block_cols)),
        out_shape=(
            jax.ShapeDtypeStruct((owned, cols * out_width), BF16),
            jax.ShapeDtypeStruct((owned, rows * in_width), BF16),
        ),
        in_specs=[pl.BlockSpec(memory_space=pltpu.SMEM)]
        + [pl.BlockSpec(memory_space=pltpu.MemorySpace.HBM)] * 7,
        out_specs=(pl.BlockSpec(memory_space=pl.ANY), pl.BlockSpec(memory_space=pl.ANY)),
        scratch_shapes=[
            pltpu.SMEM(tok_count.shape, jnp.int32),
            pltpu.VMEM(owner_order.shape, jnp.int32),
            pltpu.VMEM((1, slot_total), jnp.int32),
            pltpu.VMEM((1, slot_total), jnp.int32),
            pltpu.SMEM((1, table), jnp.int32),
            pltpu.VMEM((1, table), jnp.int32),
            pltpu.VMEM((slot_total + 1, blk, blk), BF16),
            pltpu.VMEM((tokens, in_width), BF16),
            pltpu.VMEM((tokens, in_width), BF16),
            pltpu.VMEM((rows, shard, out_width), BF16),
            pltpu.VMEM((FWD_UNITS, 2, tokens // 2, fwd_width), BF16),
            pltpu.VMEM((FWD_UNITS, tokens // 2, fwd_width), BF16),
            pltpu.VMEM((FWD_UNITS, ring, shard, fwd_width), BF16),
            pltpu.VMEM((FWD_UNITS, shard, fwd_width), BF16),
            pltpu.VMEM((FWD_UNITS, shard, fwd_width), BF16),
            pltpu.VMEM((FWD_UNITS, shard, fwd_width), BF16),
            pltpu.VMEM((FWD_UNITS, cols, owned, fwd_width), BF16),
            pltpu.VMEM((BWD_UNITS, cols, NEAR, owned, bwd_width), BF16),
            pltpu.VMEM((BWD_UNITS, NEAR, owned, bwd_width), BF16),
            pltpu.VMEM((BWD_UNITS, NEAR, owned, bwd_width), BF16),
            pltpu.VMEM((BWD_UNITS, NEAR, owned, bwd_width), BF16),
            pltpu.VMEM((BWD_UNITS // BWD_GROUP, NEAR, owned, BWD_GROUP * bwd_width), BF16),
            pltpu.VMEM((FAR_UNITS, cols, rows - NEAR, owned, far_width), BF16),
            pltpu.VMEM((FAR_UNITS, cols - 1, rows - NEAR, owned, far_width), BF16),
            pltpu.VMEM((FAR_UNITS, rows - NEAR, owned, far_width), BF16),
            dma((8,)),
            dma((13,)),
            dma((13,)),
            dma((FWD_UNITS,)),
            dma((FWD_UNITS,)),
            dma((FWD_UNITS, 3)),
            dma((FWD_UNITS, 3)),
            dma((FWD_UNITS, cols)),
            dma,
            dma((BWD_UNITS, 3)),
            dma((BWD_UNITS, 3)),
            dma((BWD_UNITS // BWD_GROUP, NEAR)),
            dma((FAR_UNITS, 5)),
            dma((FAR_UNITS, 3)),
            dma,
            pltpu.SemaphoreType.REGULAR,
        ],
        compiler_params=pltpu.CompilerParams(
            collective_id=0, has_side_effects=True, vmem_limit_bytes=32 * 1024 * 1024
        ),
    )(
        blk_count,
        *[
            pltpu.with_memory_space_constraint(operand, pltpu.MemorySpace.HBM)
            for operand in (
                tok_count,
                owner_order,
                blk_row.reshape(1, slot_total),
                blk_col.reshape(1, slot_total),
                x_fwd,
                dy_bwd,
                w_blocks.reshape(slot_total, blk, blk),
            )
        ],
    )
    section = lax.axis_index("section")
    y_next = jnp.where(section > 0, y_raw, jnp.zeros_like(y_raw))
    dx_section = jnp.where(section >= 0, dx_raw, jnp.zeros_like(dx_raw))
    return (y_next, dx_section)


def solution(mesh):
    return jax.shard_map(
        local,
        mesh=mesh,
        in_specs=(
            P("section", "row"),
            P(("section", "row"), "col"),
            P("section", "row", "col", None, None, None),
            P("section", "row", "col", None),
            P("section", "row", "col", None),
            P("section", "row", "col"),
            P("section", None),
            P("section", None),
        ),
        out_specs=(P(("section", "row", "col"), None), P(("section", "row", "col"), None)),
        check_vma=False,
    )
```
